32 devices in a mesh: dom: 8 (over y, x, core), group: 4 (over z).
Axes of the slice: x: 2, y: 2, z: 4, core: 2. Of those that a mesh axis runs over, the one named last changes fastest.
Arguments:
- nodes: bfloat16 [32, 256, 128], P(('dom', 'group')), may hold values from -6 to 6
- edges: bfloat16 [32, 1536, 128], P(('dom', 'group')), may hold values from -6 to 6
- node_cot: bfloat16 [32, 256, 128], P(('dom', 'group')), may hold values from -6 to 6
- send_index: int32 [32, 4, 128], P(('dom', 'group')), may hold values from 0 to 255
- halo_count: int32 [32, 4], P(('dom', 'group')), may hold values from 0 to 128, as said below
- senders: int32 [32, 1536], P(('dom', 'group')), may hold values from 0 to 767, as said below
- receivers: int32 [32, 1536], P(('dom', 'group')), may hold values from 0 to 255, as said below
- edge_in_w: bfloat16 [2, 384, 128], replicated, may hold values from -0.3125 to 0.3125
- edge_out_w: bfloat16 [2, 128, 128], replicated, may hold values from -0.5 to 0.5
- node_in_w: bfloat16 [2, 256, 128], replicated, may hold values from -0.375 to 0.375
- node_out_w: bfloat16 [2, 128, 128], replicated, may hold values from -0.5 to 0.5
- biases: float32 [2, 4, 128], replicated, may hold values from -3 to 3
- gains: float32 [2, 2, 128], replicated, may hold values from 0.1 to 1.9
Outputs:
- nodes_out: bfloat16 [32, 256, 128], P(('dom', 'group'))
- node_grad: bfloat16 [32, 256, 128], P(('dom', 'group'))
- edge_grad: bfloat16 [32, 1536, 128], P(('dom', 'group'))
- edge_in_grad: float32 [2, 384, 128], replicated
- edge_out_grad: float32 [2, 128, 128], replicated
- node_in_grad: float32 [2, 256, 128], replicated
- node_out_grad: float32 [2, 128, 128], replicated
- bias_grad: float32 [2, 4, 128], replicated
- gain_grad: float32 [2, 2, 128], replicated
The draws below stay inside these ranges and needn't reach their ends.
Inputs may be any that keep to these rules, and one draw needn't show every extreme that they name: `halo_count`: slot order: from the lower then the upper partition along dom, then along group; 0 exactly where that neighbour does not exist; every slot reaches 128 on some partition. `senders`: below 256: a node of the partition; 256 + s: the s-th live halo row of the table, s below the partition's total halo_count. `receivers`: never fall along a partition's edges; within each aligned block of 512 edges they span fewer than 128 nodes.
All inputs are finite; a program needn't handle non-finite values.
Results may differ from the reference program's by a relative error of at most 0.02.
Values may be sent and summed in bfloat16 or wider, within the bound.
A program may use at most 64 MiB of HBM per device.

```python
from functools import partial
import jax
import jax.numpy as jnp
from jax import lax

H = 128
L = 2
NODE_DEV = 256
HALO = 128
EDGE_DEV = 1536
PARTITIONS = 32
N_DOM = 8
N_GROUP = 4


def counts_table(key):
    base_key = jax.random.fold_in(key, 7)
    first_key, second_key = jax.random.split(base_key)
    partition = jnp.arange(PARTITIONS, dtype=jnp.int32)
    dom_place = partition // N_GROUP
    group_place = partition % N_GROUP
    present = jnp.stack([dom_place > 0, dom_place < N_DOM - 1, group_place > 0, group_place < N_GROUP - 1], axis=1)
    drawn = jax.random.randint(first_key, (PARTITIONS, 4), HALO // 4, HALO + 1)
    scores = jnp.where(present, jax.random.randint(second_key, (PARTITIONS, 4), 0, 1 << 30), -1)
    topmost = scores == jnp.max(scores, axis=0, keepdims=True)
    drawn = jnp.where(topmost, HALO, drawn)
    drawn = jnp.where((partition == N_GROUP + 1)[:, None], HALO, drawn)
    return jnp.where(present, drawn, 0).astype(jnp.int32)


def draw_halo_count(key, part):
    return counts_table(key)


def draw_senders(key, part):
    counts = counts_table(key)
    live_rows = jnp.sum(counts, axis=1).astype(jnp.int32)
    base_key = jax.random.fold_in(key, 11)
    local_key, pick_key, mode_key = jax.random.split(base_key, 3)
    local_ids = jax.random.randint(local_key, (PARTITIONS, EDGE_DEV), 0, NODE_DEV)
    picks = jax.random.randint(pick_key, (PARTITIONS, EDGE_DEV), 0, 1 << 30)
    remote_ids = NODE_DEV + picks % live_rows[:, None]
    choose_remote = jax.random.randint(mode_key, (PARTITIONS, EDGE_DEV), 0, 4) == 0
    chosen = jnp.where(choose_remote, remote_ids, local_ids).astype(jnp.int32)
    last_live = (NODE_DEV + live_rows - 1).astype(jnp.int32)
    first_edge = jnp.arange(EDGE_DEV, dtype=jnp.int32) == 0
    return jnp.where(first_edge[None, :], last_live[:, None], chosen).astype(jnp.int32)


def draw_receivers(key, part):
    base_key = jax.random.fold_in(key, 23)
    ramp_rows = jnp.arange(EDGE_DEV, dtype=jnp.int32) * NODE_DEV // EDGE_DEV
    jitter = jax.random.randint(base_key, (PARTITIONS, EDGE_DEV), 0, 32)
    return jnp.clip(jnp.sort(ramp_rows[None, :] + jitter, axis=1), 0, NODE_DEV - 1).astype(jnp.int32)


def touch_ends(array, key, least, top_value):
    index_at = [jax.random.randint(jax.random.fold_in(key, axis), (), 0, length) for axis, length in enumerate(array.shape)]
    main_axis = array.shape.index(max(array.shape))
    neighbour = index_at[:main_axis] + [(index_at[main_axis] + 1) % array.shape[main_axis]] + index_at[main_axis + 1:]
    return array.at[tuple(index_at)].set(least).at[tuple(neighbour)].set(top_value)


def levels(rng, dims, pieces, smallest, largest):
    gain, own = 1.0, jax.random.fold_in(rng, 6)
    for position, blocks in pieces:
        steps = jnp.exp(jax.random.uniform(jax.random.fold_in(own, position), (blocks,), jnp.float32, smallest / len(pieces), largest / len(pieces)))
        gain = gain * jnp.repeat(steps, dims[position] // blocks).reshape([-1 if axis == position else 1 for axis in range(len(dims))])
    return gain


def normal_values(rng, shape, width, most, shards=(), kind=jnp.bfloat16):
    gain = levels(rng, shape, shards, -0.22, 0.18) if shards else 1.0
    entries = jax.random.normal(rng, shape, jnp.float32) * width * gain
    return jnp.minimum(jnp.maximum(entries, -most), most).astype(kind)


def setup_inputs(seed: int = 0) -> dict:
    seeds = jax.random.split(jax.random.key(seed), 14)
    nodes = normal_values(seeds[0], (PARTITIONS, NODE_DEV, H), 1.0, 6.0, ((0, 32),))
    edges = normal_values(seeds[1], (PARTITIONS, EDGE_DEV, H), 1.0, 6.0, ((0, 32),))
    node_cot = normal_values(seeds[2], (PARTITIONS, NODE_DEV, H), 1.0, 6.0, ((0, 32),))
    send_index = touch_ends(jax.random.randint(seeds[3], (PARTITIONS, 4, HALO), 0, NODE_DEV), jax.random.fold_in(seeds[3], 1), 0, NODE_DEV - 1).astype(jnp.int32)
    halo_count = draw_halo_count(jax.random.fold_in(seeds[13], 71), 0)
    senders = draw_senders(jax.random.fold_in(seeds[13], 71), 0)
    receivers = draw_receivers(jax.random.fold_in(seeds[13], 71), 0)
    edge_in_w = normal_values(seeds[7], (L, 3 * H, H), (3 * H) ** -0.5, 0.3125)
    edge_out_w = normal_values(seeds[8], (L, H, H), H ** -0.5, 0.5)
    node_in_w = normal_values(seeds[9], (L, 2 * H, H), (2 * H) ** -0.5, 0.375)
    node_out_w = normal_values(seeds[10], (L, H, H), H ** -0.5, 0.5)
    biases = normal_values(seeds[11], (L, 4, H), 0.5, 3.0, (), jnp.float32)
    gains = jnp.clip(1.0 + 0.18 * jax.random.normal(seeds[12], (L, 2, H), jnp.float32), 0.1, 1.9)
    return dict(nodes=nodes, edges=edges, node_cot=node_cot, send_index=send_index, halo_count=halo_count, senders=senders, receivers=receivers, edge_in_w=edge_in_w, edge_out_w=edge_out_w, node_in_w=node_in_w, node_out_w=node_out_w, biases=biases, gains=gains)


def norm_rows(values, gain_row):
    centre = values - lax.optimization_barrier(jnp.mean(values, axis=-1, keepdims=True))
    spread = lax.optimization_barrier(jnp.mean(centre * centre, axis=-1, keepdims=True))
    return centre * lax.rsqrt(spread + 1e-05) * gain_row

def pack_halo(received, counts):
    halo_depth = received.shape[1]
    feat_width = received.shape[2]
    block_ends = jnp.cumsum(counts).astype(jnp.int32)
    block_starts = (block_ends - counts).astype(jnp.int32)
    positions = jnp.arange(4 * halo_depth, dtype=jnp.int32)
    block_of = lax.optimization_barrier(jnp.sum((positions[:, None] >= block_ends[None, :]).astype(jnp.int32), axis=1)).astype(jnp.int32)
    clamped = jnp.minimum(block_of, 3)
    selector = jnp.arange(4, dtype=jnp.int32)
    offsets = lax.optimization_barrier(jnp.sum(jnp.where(clamped[:, None] == selector[None, :], block_starts[None, :], 0), axis=1)).astype(jnp.int32)
    within_block = positions - offsets
    sources = clamped * halo_depth + jnp.clip(within_block, 0, halo_depth - 1)
    picked = received.reshape(4 * halo_depth, feat_width)[sources]
    return jnp.where((block_of < 4)[:, None], picked, jnp.zeros_like(picked))

def edge_update(weights, edge_rows, sent_feat, recv_feat):
    edge_in, edge_out, node_in, node_out, bias_rows, gain_rows = weights
    joined = jnp.concatenate([edge_rows, sent_feat, recv_feat], axis=1)
    hidden = jax.nn.silu(jnp.dot(joined, edge_in, preferred_element_type=jnp.float32) + bias_rows[0]).astype(jnp.bfloat16)
    mapped = jnp.dot(hidden, edge_out, preferred_element_type=jnp.float32) + bias_rows[1]
    return (edge_rows.astype(jnp.float32) + norm_rows(mapped, gain_rows[0])).astype(jnp.bfloat16)

def node_update(weights, node_vals, summed):
    edge_in, edge_out, node_in, node_out, bias_rows, gain_rows = weights
    joined = jnp.concatenate([node_vals.astype(jnp.bfloat16), summed.astype(jnp.bfloat16)], axis=1)
    hidden = jax.nn.silu(jnp.dot(joined, node_in, preferred_element_type=jnp.float32) + bias_rows[2]).astype(jnp.bfloat16)
    mapped = jnp.dot(hidden, node_out, preferred_element_type=jnp.float32) + bias_rows[3]
    return (node_vals + norm_rows(mapped, gain_rows[1])).astype(jnp.bfloat16)

def local_layer(weights, edge_rows, node_vals, received, counts, sender_ids, receiver_ids):
    table = jnp.concatenate([node_vals, pack_halo(received, counts)], axis=0)
    sent_feat = table[sender_ids].astype(jnp.bfloat16)
    recv_feat = table[receiver_ids].astype(jnp.bfloat16)
    edge_new = edge_update(weights, edge_rows, sent_feat, recv_feat)
    summed = jax.ops.segment_sum(edge_new.astype(jnp.float32), receiver_ids, num_segments=node_vals.shape[0])
    return (edge_new, node_update(weights, node_vals, summed))

def gather_rows(node_rows, send_rows):
    return node_rows.astype(jnp.float32)[send_rows]

def exchange_rows(node_all, send_index):
    sent_rows = jax.vmap(gather_rows)(node_all, send_index)
    grid_rows = sent_rows.reshape((N_DOM, N_GROUP) + sent_rows.shape[1:])
    zero_dom = jnp.zeros_like(grid_rows[:1, :, 0])
    zero_grp = jnp.zeros_like(grid_rows[:, :1, 0])
    slot_zero = jnp.concatenate([zero_dom, grid_rows[:-1, :, 0]], axis=0)
    slot_one = jnp.concatenate([grid_rows[1:, :, 1], zero_dom], axis=0)
    slot_two = jnp.concatenate([zero_grp, grid_rows[:, :-1, 2]], axis=1)
    slot_three = jnp.concatenate([grid_rows[:, 1:, 3], zero_grp], axis=1)
    return jnp.stack([slot_zero, slot_one, slot_two, slot_three], axis=2).reshape(sent_rows.shape)

def add_rows(returned, send_rows, node_count):
    return jax.ops.segment_sum(returned.reshape(-1, returned.shape[-1]), send_rows.reshape(-1), num_segments=node_count)

def scatter_back(cot_all, send_index, node_count):
    grid_rows = cot_all.reshape((N_DOM, N_GROUP) + cot_all.shape[1:])
    zero_dom = jnp.zeros_like(grid_rows[:1, :, 0])
    zero_grp = jnp.zeros_like(grid_rows[:, :1, 0])
    back_zero = jnp.concatenate([grid_rows[1:, :, 0], zero_dom], axis=0)
    back_one = jnp.concatenate([zero_dom, grid_rows[:-1, :, 1]], axis=0)
    back_two = jnp.concatenate([grid_rows[:, 1:, 2], zero_grp], axis=1)
    back_three = jnp.concatenate([zero_grp, grid_rows[:, :-1, 3]], axis=1)
    returned = jnp.stack([back_zero, back_one, back_two, back_three], axis=2).reshape(cot_all.shape)
    return jax.vmap(partial(add_rows, node_count=node_count))(returned, send_index)

def reference(nodes, edges, node_cot, send_index, halo_count, senders, receivers, edge_in_w, edge_out_w, node_in_w, node_out_w, biases, gains):
    layer_count = edge_in_w.shape[0]
    node_count = nodes.shape[1]
    node_all = nodes
    edge_all = edges
    saved_inputs = []
    for layer_index in range(layer_count):
        weights = (edge_in_w[layer_index], edge_out_w[layer_index], node_in_w[layer_index], node_out_w[layer_index], biases[layer_index], gains[layer_index])
        received = exchange_rows(node_all, send_index)
        saved_inputs.append((edge_all, node_all, received))

        def forward_one(carried, members, weights=weights):
            edge_vals, node_vals, halo_vals, counts, sender_ids, receiver_ids = members
            return (carried, local_layer(weights, edge_vals, node_vals.astype(jnp.float32), halo_vals, counts, sender_ids, receiver_ids))
        unused, (edge_all, node_all) = lax.scan(forward_one, jnp.zeros((), jnp.int32), (edge_all, node_all, received, halo_count, senders, receivers))
    node_cot_all = node_cot
    edge_cot_all = jnp.zeros_like(edges)
    layer_grads = [None] * layer_count
    for layer_index in reversed(range(layer_count)):
        weights = (edge_in_w[layer_index], edge_out_w[layer_index], node_in_w[layer_index], node_out_w[layer_index], biases[layer_index], gains[layer_index])
        edge_in_all, node_in_all, received = saved_inputs[layer_index]

        def backward_one(totals, members, weights=weights):
            edge_vals, node_vals, halo_vals, counts, sender_ids, receiver_ids, edge_cot, node_cot_rows = members

            def layer_call(params, edge_arg, node_arg, halo_arg):
                return local_layer(params, edge_arg, node_arg, halo_arg, counts, sender_ids, receiver_ids)
            outputs, pullback = jax.vjp(layer_call, weights, edge_vals, node_vals.astype(jnp.float32), halo_vals)
            weight_cot, edge_back, node_back, halo_back = pullback((edge_cot, node_cot_rows))
            totals = tuple((running + leaf_val.astype(jnp.float32) for running, leaf_val in zip(totals, weight_cot)))
            return (totals, (edge_back, node_back, halo_back))
        initial = tuple((jnp.zeros(leaf_val.shape, jnp.float32) for leaf_val in weights))
        totals, (edge_cot_all, node_back_all, halo_back_all) = lax.scan(backward_one, initial, (edge_in_all, node_in_all, received, halo_count, senders, receivers, edge_cot_all, node_cot_all))
        node_back_all = node_back_all + scatter_back(halo_back_all, send_index, node_count)
        node_cot_all = node_back_all.astype(jnp.bfloat16)
        layer_grads[layer_index] = totals
    grad_scale = (N_DOM * N_GROUP * node_count) ** (-0.5)
    stacked = tuple((jnp.stack([layer_grads[layer_index][member] for layer_index in range(layer_count)]) * grad_scale for member in range(6)))
    return (node_all, node_cot_all, edge_cot_all, stacked[0], stacked[1], stacked[2], stacked[3], stacked[4], stacked[5])
```

```python
import functools

import jax
import jax.numpy as jnp
from jax import lax
from jax.experimental import pallas as pl
from jax.experimental.pallas import tpu as pltpu
from jax.sharding import PartitionSpec as P

F32 = jnp.float32
BF16 = jnp.bfloat16
MESH = pl.DeviceIdType.MESH


def mm(a, b):
    return lax.dot_general(a, b, (((1,), (0,)), ((), ())), preferred_element_type=F32)


def mm_nt(a, b):
    return lax.dot_general(a, b, (((1,), (1,)), ((), ())), preferred_element_type=F32)


def fold(x):
    return jnp.sum(x.reshape(x.shape[0] // 8, 8, x.shape[1]), axis=0)


def row_sum(x):
    return jnp.sum(x, axis=0, keepdims=True)


def norm_parts(values):
    centre = values - jnp.mean(values, axis=-1, keepdims=True)
    spread = jnp.mean(centre * centre, axis=-1, keepdims=True)
    inv = lax.rsqrt(spread + 1e-05)
    return centre * inv, inv


def norm_back(cot, gain_row, hat, inv):
    u = cot * gain_row
    return inv * (
        u
        - jnp.mean(u, axis=-1, keepdims=True)
        - hat * jnp.mean(u * hat, axis=-1, keepdims=True)
    )


def silu_parts(pre):
    sig = 1.0 / (1.0 + jnp.exp(-pre))
    return (pre * sig).astype(BF16), sig * (1.0 + pre * (1.0 - sig))


def kernel(
    dims,
    cnt,
    nodes,
    edges,
    ncot,
    sidx,
    snd,
    rcv,
    w1,
    w2,
    n1,
    n2,
    bias,
    gain,
    x_out,
    x_grad,
    e_grad,
    g_w1,
    g_w2,
    g_n1,
    g_n2,
    g_b,
    g_g,
    o_s,
    ot_s,
    o_r,
    ot_r,
    o_x,
    ot_x,
    tab,
    e_in,
    e_last,
    sq,
    hid,
    slope,
    hat,
    inv,
    jn,
    nhid,
    nslope,
    nhat,
    ninv,
    dm,
    dp,
    de,
    dsq,
    dx,
    dab,
    fsrc,
    bsrc,
    ret,
    grads,
    buf_a,
    buf_b,
    gat,
    fs,
    fr,
    bs,
    br,
    a_s,
    a_r,
    b_s,
    b_r,
    c_s,
    c_r,
):
    D, G, L, N, E, H, HALO, C, share = dims
    d = lax.axis_index("dom")
    g = lax.axis_index("group")
    rows_w = 7 * H

    has_up = d + 1 < D
    has_down = d > 0
    has_right = g + 1 < G
    has_left = g > 0
    out_ok = (has_up, has_down, has_right, has_left)
    in_ok = (has_down, has_up, has_left, has_right)
    out_dev = ({"dom": d + 1}, {"dom": d - 1}, {"group": g + 1}, {"group": g - 1})
    in_dev = ({"dom": d - 1}, {"dom": d + 1}, {"group": g - 1}, {"group": g + 1})

    def fcopy(l, k):
        return pltpu.make_async_remote_copy(
            src_ref=fsrc.at[l, pl.ds(k * HALO, HALO)],
            dst_ref=tab.at[l, pl.ds(N + k * HALO, HALO)],
            send_sem=fs.at[l, k],
            recv_sem=fr.at[l, k],
            device_id=out_dev[k],
            device_id_type=MESH,
        )

    def bcopy(l, k):
        return pltpu.make_async_remote_copy(
            src_ref=bsrc.at[l, pl.ds(k * HALO, HALO)],
            dst_ref=ret.at[l, pl.ds(k * HALO, HALO)],
            send_sem=bs.at[l, k],
            recv_sem=br.at[l, k],
            device_id=in_dev[k],
            device_id_type=MESH,
        )

    def send_halo(l):
        for k in range(4):
            @pl.when(out_ok[k])
            def _(k=k):
                fcopy(l, k).start()

    def wait_halo(l):
        for k in range(4):
            @pl.when(in_ok[k])
            def _(k=k):
                fcopy(l, k).wait_recv()

    def send_ret(l):
        for k in range(4):
            @pl.when(in_ok[k])
            def _(k=k):
                bcopy(l, k).start()

    def wait_ret(l):
        for k in range(4):
            @pl.when(out_ok[k])
            def _(k=k):
                bcopy(l, k).wait_recv()

    def acopy(l, off):
        peer = lax.rem(d + off, D)
        return pltpu.make_async_remote_copy(
            src_ref=grads.at[l, pl.ds(pl.multiple_of(peer * share, share), share)],
            dst_ref=buf_a.at[l, off - 1],
            send_sem=a_s.at[l, off - 1],
            recv_sem=a_r.at[l, off - 1],
            device_id={"dom": peer},
            device_id_type=MESH,
        )

    def b_copy(l, off):
        peer = lax.rem(g + off, G)
        return pltpu.make_async_remote_copy(
            src_ref=buf_b.at[l, g],
            dst_ref=buf_b.at[l, g],
            send_sem=b_s.at[l, off - 1],
            recv_sem=b_r.at[l, off - 1],
            device_id={"group": peer},
            device_id_type=MESH,
        )

    def c_copy(l, off):
        peer = lax.rem(d + off, D)
        mine = pl.ds(pl.multiple_of(d * share, share), share)
        return pltpu.make_async_remote_copy(
            src_ref=gat.at[l, mine],
            dst_ref=gat.at[l, mine],
            send_sem=c_s.at[l, off - 1],
            recv_sem=c_r.at[l, off - 1],
            device_id={"dom": peer},
            device_id_type=MESH,
        )

    for l in range(L):
        tab[l, N:, :] = jnp.zeros((4 * HALO, H), BF16)
        ret[l] = jnp.zeros((4 * HALO, H), BF16)
    barrier = pltpu.get_barrier_semaphore()
    for off in range(1, D):
        pl.semaphore_signal(
            barrier, inc=1, device_id={"dom": lax.rem(d + off, D)}, device_id_type=MESH
        )
    for off in range(1, G):
        pl.semaphore_signal(
            barrier, inc=1, device_id={"group": lax.rem(g + off, G)}, device_id_type=MESH
        )

    def spread_column(row):
        return jnp.broadcast_to(row, (128, row.shape[1])).T

    def one_hot(column, width, ref, row0):
        rows = column.shape[0]
        lane = lax.broadcasted_iota(jnp.int32, (rows, 128), 1)
        for j in range(width // 128):
            ref[row0 : row0 + rows, j * 128 : (j + 1) * 128] = (
                (column - 128 * j == lane).astype(F32).astype(BF16)
            )

    def one_hot_t(row, height, ref, col0):
        cols = row.shape[1]
        sub = lax.broadcasted_iota(jnp.int32, (128, cols), 0)
        for j in range(height // 128):
            ref[j * 128 : (j + 1) * 128, col0 : col0 + cols] = (
                (row - 128 * j == sub).astype(F32).astype(BF16)
            )

    x0 = nodes[0]
    tab[0, :N, :] = x0
    for k in range(4):
        one_hot(spread_column(sidx[0, k : k + 1, :]), N, o_x, k * HALO)
    fsrc[0] = mm(o_x[...], x0).astype(BF16)
    pl.semaphore_wait(barrier, D - 1 + G - 1)
    send_halo(0)

    for k in range(4):
        one_hot_t(sidx[0, k : k + 1, :], N, ot_x, k * HALO)
    sids = snd[...]
    past = sids - N
    edge_0 = cnt[0, 0]
    edge_1 = edge_0 + cnt[0, 1]
    edge_2 = edge_1 + cnt[0, 2]
    sids = (
        sids
        + jnp.where(past >= edge_0, HALO - cnt[0, 0], 0)
        + jnp.where(past >= edge_1, HALO - cnt[0, 1], 0)
        + jnp.where(past >= edge_2, HALO - cnt[0, 2], 0)
    )
    rids = rcv[...]
    for i in range(E // 256):
        part = slice(i * 256, (i + 1) * 256)
        one_hot(spread_column(rids[:, part]), N, o_r, i * 256)
        one_hot(spread_column(sids[:, part]), N + 4 * HALO, o_s, i * 256)
        one_hot_t(rids[:, part], N, ot_r, i * 256)
        one_hot_t(sids[:, part], N + 4 * HALO, ot_s, i * 256)

    for l in range(L):
        wait_halo(l)

        def edge_step(i, carry, l=l):
            rows = pl.ds(pl.multiple_of(i * C, C), C)
            e_rows = edges[0, rows, :] if l == 0 else e_in[l - 1, rows, :]
            s_rows = mm(o_s[rows, :], tab[l]).astype(BF16)
            q_rows = mm(o_r[rows, :], tab[l, :N, :]).astype(BF16)
            pair = jnp.concatenate([s_rows, q_rows], axis=1)
            sq[l, rows, :] = pair
            pre = mm(e_rows, w1[l, :H, :]) + mm(pair, w1[l, H:, :]) + bias[l, 0:1, :]
            h_rows, sl = silu_parts(pre)
            hid[l, rows, :] = h_rows
            slope[l, rows, :] = sl
            hat_rows, inv_rows = norm_parts(mm(h_rows, w2[l]) + bias[l, 1:2, :])
            hat[l, rows, :] = hat_rows
            inv[l, rows, :] = jnp.broadcast_to(inv_rows, hat_rows.shape)
            new = (e_rows.astype(F32) + hat_rows * gain[l, 0:1, :]).astype(BF16)
            if l + 1 < L:
                e_in[l, rows, :] = new
            else:
                e_last[rows, :] = new
            return carry

        lax.fori_loop(0, E // C, edge_step, 0)
        e_new = e_in[l] if l + 1 < L else e_last[...]
        x_rows = tab[l, :N, :]
        joined = jnp.concatenate([x_rows, mm(ot_r[...], e_new).astype(BF16)], axis=1)
        jn[l] = joined
        h_rows, sl = silu_parts(mm(joined, n1[l]) + bias[l, 2:3, :])
        nhid[l] = h_rows
        nslope[l] = sl
        hat_rows, inv_rows = norm_parts(mm(h_rows, n2[l]) + bias[l, 3:4, :])
        nhat[l] = hat_rows
        ninv[l] = jnp.broadcast_to(inv_rows, hat_rows.shape)
        x_new = (x_rows.astype(F32) + hat_rows * gain[l, 1:2, :]).astype(BF16)
        if l + 1 < L:
            tab[l + 1, :N, :] = x_new
            fsrc[l + 1] = mm(o_x[...], x_new).astype(BF16)
            send_halo(l + 1)
        else:
            x_out[0] = x_new

    for l in reversed(range(L)):
        cot = ncot[0].astype(F32) if l == L - 1 else x_cot.astype(F32)
        nh = nhat[l]
        dgn = fold(cot * nh)
        dmn = norm_back(cot, gain[l, 1:2, :], nh, ninv[l])
        dbn2 = fold(dmn)
        dmn = dmn.astype(BF16)
        dpn = mm_nt(dmn, n2[l]).astype(BF16).astype(F32) * nslope[l]
        dbn1 = fold(dpn)
        dpn = dpn.astype(BF16)
        djn = mm_nt(dpn, n1[l]).astype(BF16)
        dx[...] = cot + djn[:, :H].astype(F32)
        dab[...] = djn[:, H:]

        def edge_back(i, carry, l=l):
            s_g, s_b2, s_b1 = carry
            rows = pl.ds(pl.multiple_of(i * C, C), C)
            c_rows = mm(o_r[rows, :], dab[...])
            if l < L - 1:
                c_rows = (de[rows, :].astype(F32) + c_rows).astype(BF16).astype(F32)
            hat_rows = hat[l, rows, :]
            dm_rows = norm_back(c_rows, gain[l, 0:1, :], hat_rows, inv[l, rows, :])
            s_g = s_g + fold(c_rows * hat_rows)
            s_b2 = s_b2 + fold(dm_rows)
            dm_b = dm_rows.astype(BF16)
            dm[rows, :] = dm_b
            dp_rows = mm_nt(dm_b, w2[l]).astype(BF16).astype(F32) * slope[l, rows, :]
            s_b1 = s_b1 + fold(dp_rows)
            dp_b = dp_rows.astype(BF16)
            dp[rows, :] = dp_b
            dj = mm_nt(dp_b, w1[l]).astype(BF16)
            back = (c_rows + dj[:, :H].astype(F32)).astype(BF16)
            if l == 0:
                e_grad[0, rows, :] = back
            else:
                de[rows, :] = back
            dsq[rows, :] = dj[:, H:]
            return s_g, s_b2, s_b1

        zero = jnp.zeros((8, H), F32)
        dge, dbe2, dbe1 = lax.fori_loop(0, E // C, edge_back, (zero, zero, zero))
        bsrc[l] = mm(ot_s[N:, :], dsq[:, :H]).astype(BF16)
        send_ret(l)

        def put(first, value):
            grads[l, first : first + value.shape[0], :] = value.astype(BF16)

        dp_t = dp[...].T
        e_rows = edges[0] if l == 0 else e_in[l - 1]
        put(0, mm(dp_t, e_rows).T)
        put(H, mm(dp_t, sq[l]).T)
        put(3 * H, mm(dm[...].T, hid[l]).T)
        put(4 * H, mm(dpn.T, jn[l]).T)
        put(6 * H, mm(dmn.T, nhid[l]).T)
        small = [row_sum(v) for v in (dbe1, dbe2, dbn1, dbn2, dge, dgn)]
        put(
            rows_w,
            jnp.concatenate(small + [jnp.zeros((D * share - rows_w - 6, H), F32)], axis=0),
        )
        for off in range(1, D):
            acopy(l, off).start()
        total = dx[...] + mm(ot_s[:N, :], dsq[:, :H]) + mm(ot_r[...], dsq[:, H:])
        wait_ret(l)
        x_cot = (total + mm(ot_x[...], ret[l])).astype(BF16)
    x_grad[0] = x_cot

    mine = pl.ds(pl.multiple_of(d * share, share), share)
    for l in reversed(range(L)):
        acc = grads[l, mine, :].astype(F32)
        for off in range(1, D):
            acopy(l, off).wait_recv()
            acc = acc + buf_a[l, off - 1].astype(F32)
        buf_b[l, g] = acc.astype(BF16)
        for off in range(1, G):
            b_copy(l, off).start()
    for l in reversed(range(L)):
        for off in range(1, G):
            b_copy(l, off).wait_recv()
        acc = buf_b[l, 0].astype(F32)
        for i in range(1, G):
            acc = acc + buf_b[l, i].astype(F32)
        gat[l, mine, :] = acc.astype(BF16)
        for off in range(1, D):
            c_copy(l, off).start()
    scale = (D * G * N) ** (-0.5)
    for l in reversed(range(L)):
        for off in range(1, D):
            c_copy(l, off).wait_recv()

        def take(first, count):
            return gat[l, first : first + count, :].astype(F32) * scale

        g_w1[l] = take(0, 3 * H)
        g_w2[l] = take(3 * H, H)
        g_n1[l] = take(4 * H, 2 * H)
        g_n2[l] = take(6 * H, H)
        tail = take(rows_w, 16)
        g_b[l] = tail[:4]
        g_g[l] = tail[4:6]

    for l in range(L):
        for k in range(4):
            @pl.when(out_ok[k])
            def _(k=k, l=l):
                fcopy(l, k).wait_send()

            @pl.when(in_ok[k])
            def _(k=k, l=l):
                bcopy(l, k).wait_send()
        for off in range(1, D):
            acopy(l, off).wait_send()
            c_copy(l, off).wait_send()
        for off in range(1, G):
            b_copy(l, off).wait_send()


def shards(D, G, nodes, edges, node_cot, send_index, halo_count, senders, receivers, *weights):
    edge_in_w, edge_out_w, node_in_w, node_out_w, biases, gains = weights
    _, N, H = nodes.shape
    E = edges.shape[1]
    L = edge_in_w.shape[0]
    HALO = send_index.shape[2]
    C = 256
    rows = 7 * H + 6
    share = -(-rows // (16 * D)) * 16
    dims = (D, G, L, N, E, H, HALO, C, share)
    T = N + 4 * HALO
    R = D * share
    out_shape = (
        jax.ShapeDtypeStruct(nodes.shape, BF16),
        jax.ShapeDtypeStruct(nodes.shape, BF16),
        jax.ShapeDtypeStruct(edges.shape, BF16),
        jax.ShapeDtypeStruct(edge_in_w.shape, F32),
        jax.ShapeDtypeStruct(edge_out_w.shape, F32),
        jax.ShapeDtypeStruct(node_in_w.shape, F32),
        jax.ShapeDtypeStruct(node_out_w.shape, F32),
        jax.ShapeDtypeStruct(biases.shape, F32),
        jax.ShapeDtypeStruct(gains.shape, F32),
    )
    V = pltpu.VMEM
    dma = pltpu.SemaphoreType.DMA
    scratch = [
        V((E, T), BF16),
        V((T, E), BF16),
        V((E, N), BF16),
        V((N, E), BF16),
        V((4 * HALO, N), BF16),
        V((N, 4 * HALO), BF16),
        V((L, T, H), BF16),
        V((max(L - 1, 1), E, H), BF16),
        V((E, H), BF16),
        V((L, E, 2 * H), BF16),
        V((L, E, H), BF16),
        V((L, E, H), F32),
        V((L, E, H), F32),
        V((L, E, H), F32),
        V((L, N, 2 * H), BF16),
        V((L, N, H), BF16),
        V((L, N, H), F32),
        V((L, N, H), F32),
        V((L, N, H), F32),
        V((E, H), BF16),
        V((E, H), BF16),
        V((E, H), BF16),
        V((E, 2 * H), BF16),
        V((N, H), F32),
        V((N, H), BF16),
        V((L, 4 * HALO, H), BF16),
        V((L, 4 * HALO, H), BF16),
        V((L, 4 * HALO, H), BF16),
        V((L, R, H), BF16),
        V((L, max(D - 1, 1), share, H), BF16),
        V((L, G, share, H), BF16),
        V((L, R, H), BF16),
        dma((L, 4)),
        dma((L, 4)),
        dma((L, 4)),
        dma((L, 4)),
        dma((L, D)),
        dma((L, D)),
        dma((L, G)),
        dma((L, G)),
        dma((L, D)),
        dma((L, D)),
    ]
    vm = pl.BlockSpec(memory_space=pltpu.VMEM)
    sm = pl.BlockSpec(memory_space=pltpu.SMEM)
    return pl.pallas_call(
        functools.partial(kernel, dims),
        out_shape=out_shape,
        in_specs=[sm] + [vm] * 12,
        out_specs=tuple([vm] * 9),
        scratch_shapes=scratch,
        compiler_params=pltpu.CompilerParams(
            collective_id=0, has_side_effects=True, vmem_limit_bytes=56 * 1024 * 1024
        ),
    )(
        halo_count,
        nodes,
        edges,
        node_cot,
        send_index,
        senders,
        receivers,
        *weights,
    )


def solution(mesh):
    part3 = P(("dom", "group"), None, None)
    part2 = P(("dom", "group"), None)
    in_specs = (part3, part3, part3, part3, part2, part2, part2) + (P(),) * 6
    out_specs = (part3, part3, part3) + (P(),) * 6
    body = functools.partial(shards, mesh.shape["dom"], mesh.shape["group"])
    return jax.shard_map(
        body, mesh=mesh, in_specs=in_specs, out_specs=out_specs, check_vma=False
    )
```

```python
import functools

import jax
import jax.numpy as jnp
from jax import lax
from jax.experimental import pallas as pl
from jax.experimental.pallas import tpu as pltpu
from jax.sharding import PartitionSpec as P

F32 = jnp.float32
BF16 = jnp.bfloat16
MESH = pl.DeviceIdType.MESH
VMEM_MAIN = 58 * 1024 * 1024


def mm(a, b):
    return lax.dot_general(a, b, (((1,), (0,)), ((), ())), preferred_element_type=F32)


def mm_nt(a, b):
    return lax.dot_general(a, b, (((1,), (1,)), ((), ())), preferred_element_type=F32)


def fold(x):
    return jnp.sum(x.reshape(x.shape[0] // 8, 8, x.shape[1]), axis=0)


def row_sum(x):
    return jnp.sum(x, axis=0, keepdims=True)


def norm_parts(values):
    centre = values - jnp.mean(values, axis=-1, keepdims=True)
    spread = jnp.mean(centre * centre, axis=-1, keepdims=True)
    inv = lax.rsqrt(spread + 1e-05)
    return centre * inv, inv


def norm_back(cot, gain_row, hat, inv):
    u = cot * gain_row
    return inv * (
        u
        - jnp.mean(u, axis=-1, keepdims=True)
        - hat * jnp.mean(u * hat, axis=-1, keepdims=True)
    )


def silu_parts(pre):
    sig = 1.0 / (1.0 + jnp.exp(-pre))
    return (pre * sig).astype(BF16), sig * (1.0 + pre * (1.0 - sig))


def kernel(
    dims,
    cnt_h,
    nodes_h,
    edges_h,
    ncot_h,
    sidx_h,
    snd_h,
    rcv_h,
    w1_h,
    w2_h,
    n1_h,
    n2_h,
    bias_h,
    gain_h,
    x_out,
    x_grad,
    e_grad,
    sum_n,
    sum_e,
    o_s,
    ot_s,
    o_r,
    ot_r,
    o_x,
    ot_x,
    tab,
    e_in,
    e_last,
    sq,
    hid,
    slope,
    hat,
    inv,
    jn,
    nhid,
    nslope,
    nhat,
    ninv,
    dm,
    dp,
    de,
    dsq,
    dx,
    dab,
    fsrc,
    bsrc,
    ret,
    grads_n,
    buf_an,
    buf_bn,
    gat_n,
    grads_e,
    buf_ae,
    buf_be,
    gat_e,
    fs,
    fr,
    bs,
    br,
    a_s,
    a_r,
    b_s,
    b_r,
    c_s,
    c_r,
    cnt,
    nodes,
    edges,
    ncot,
    sidx,
    snd,
    rcv,
    w1,
    w2,
    n1,
    n2,
    bias,
    gain,
    in_sem,
):
    D, G, L, N, E, H, HALO, C, share_n, share_e = dims
    shares = (share_n, share_e)
    grads = (grads_n, grads_e)
    buf_a = (buf_an, buf_ae)
    buf_b = (buf_bn, buf_be)
    gat = (gat_n, gat_e)
    sums = (sum_n, sum_e)
    loads = [
        pltpu.make_async_copy(src, dst, in_sem.at[i])
        for i, (src, dst) in enumerate(
            (
                (nodes_h, nodes),
                (sidx_h, sidx),
                (snd_h, snd),
                (rcv_h, rcv),
                (cnt_h, cnt),
                (edges_h, edges),
                (w1_h, w1),
                (w2_h, w2),
                (bias_h, bias),
                (gain_h, gain),
                (n1_h, n1),
                (n2_h, n2),
                (ncot_h, ncot),
            )
        )
    ]
    for load in loads:
        load.start()
    d = lax.axis_index("dom")
    g = lax.axis_index("group")

    has_up = d + 1 < D
    has_down = d > 0
    has_right = g + 1 < G
    has_left = g > 0
    out_ok = (has_up, has_down, has_right, has_left)
    in_ok = (has_down, has_up, has_left, has_right)
    out_dev = ({"dom": d + 1}, {"dom": d - 1}, {"group": g + 1}, {"group": g - 1})
    in_dev = ({"dom": d - 1}, {"dom": d + 1}, {"group": g - 1}, {"group": g + 1})

    def fcopy(l, k):
        return pltpu.make_async_remote_copy(
            src_ref=fsrc.at[l, pl.ds(k * HALO, HALO)],
            dst_ref=tab.at[l, pl.ds(N + k * HALO, HALO)],
            send_sem=fs.at[l, k],
            recv_sem=fr.at[l, k],
            device_id=out_dev[k],
            device_id_type=MESH,
        )

    def bcopy(l, k):
        return pltpu.make_async_remote_copy(
            src_ref=bsrc.at[l, pl.ds(k * HALO, HALO)],
            dst_ref=ret.at[l, pl.ds(k * HALO, HALO)],
            send_sem=bs.at[l, k],
            recv_sem=br.at[l, k],
            device_id=in_dev[k],
            device_id_type=MESH,
        )

    def send_halo(l):
        for k in range(4):
            @pl.when(out_ok[k])
            def _(k=k):
                fcopy(l, k).start()

    def wait_halo(l):
        for k in range(4):
            @pl.when(in_ok[k])
            def _(k=k):
                fcopy(l, k).wait_recv()

    def send_ret(l):
        for k in range(4):
            @pl.when(in_ok[k])
            def _(k=k):
                bcopy(l, k).start()

    def wait_ret(l):
        for k in range(4):
            @pl.when(out_ok[k])
            def _(k=k):
                bcopy(l, k).wait_recv()

    def a_copy(t, l, off):
        peer = lax.rem(d + off, D)
        return pltpu.make_async_remote_copy(
            src_ref=grads[t].at[l, peer],
            dst_ref=buf_a[t].at[l, off - 1],
            send_sem=a_s.at[t, l, off - 1],
            recv_sem=a_r.at[t, l, off - 1],
            device_id={"dom": peer},
            device_id_type=MESH,
        )

    def b_copy(t, l, off):
        return pltpu.make_async_remote_copy(
            src_ref=buf_b[t].at[l, g],
            dst_ref=buf_b[t].at[l, g],
            send_sem=b_s.at[t, l, off - 1],
            recv_sem=b_r.at[t, l, off - 1],
            device_id={"group": lax.rem(g + off, G)},
            device_id_type=MESH,
        )

    def c_copy(t, l, off):
        return pltpu.make_async_remote_copy(
            src_ref=gat[t].at[l, d],
            dst_ref=gat[t].at[l, d],
            send_sem=c_s.at[t, l, off - 1],
            recv_sem=c_r.at[t, l, off - 1],
            device_id={"dom": lax.rem(d + off, D)},
            device_id_type=MESH,
        )

    def start_a(t, l, pieces):
        rows = sum(p.shape[0] for p in pieces)
        pad = jnp.zeros((D * shares[t] - rows, H), F32)
        whole = jnp.concatenate(list(pieces) + [pad], axis=0)
        grads[t][l] = whole.reshape(D, shares[t], H).astype(BF16)
        for off in range(1, D):
            a_copy(t, l, off).start()

    def start_b(t, l):
        acc = grads[t][l, d].astype(F32)
        for off in range(1, D):
            a_copy(t, l, off).wait_recv()
            acc = acc + buf_a[t][l, off - 1].astype(F32)
        buf_b[t][l, g] = acc.astype(BF16)
        for off in range(1, G):
            b_copy(t, l, off).start()

    def start_c(t, l):
        for off in range(1, G):
            b_copy(t, l, off).wait_recv()
        acc = buf_b[t][l, 0].astype(F32)
        for i in range(1, G):
            acc = acc + buf_b[t][l, i].astype(F32)
        gat[t][l, d] = acc.astype(BF16)
        for off in range(1, D):
            c_copy(t, l, off).start()

    def end_c(t, l):
        for off in range(1, D):
            c_copy(t, l, off).wait_recv()
        sums[t][l] = gat[t][l]

    for l in range(L):
        tab[l, N:, :] = jnp.zeros((4 * HALO, H), BF16)
        ret[l] = jnp.zeros((4 * HALO, H), BF16)
    barrier = pltpu.get_barrier_semaphore()
    for off in range(1, D):
        pl.semaphore_signal(
            barrier, inc=1, device_id={"dom": lax.rem(d + off, D)}, device_id_type=MESH
        )
    for off in range(1, G):
        pl.semaphore_signal(
            barrier, inc=1, device_id={"group": lax.rem(g + off, G)}, device_id_type=MESH
        )

    def spread_column(row):
        return jnp.broadcast_to(row, (128, row.shape[1])).T

    def one_hot(column, width, ref, row0):
        rows = column.shape[0]
        lane = lax.broadcasted_iota(jnp.int32, (rows, 128), 1)
        for j in range(width // 128):
            ref[row0 : row0 + rows, j * 128 : (j + 1) * 128] = (
                (column - 128 * j == lane).astype(F32).astype(BF16)
            )

    def one_hot_t(row, height, ref, col0):
        cols = row.shape[1]
        sub = lax.broadcasted_iota(jnp.int32, (128, cols), 0)
        for j in range(height // 128):
            ref[j * 128 : (j + 1) * 128, col0 : col0 + cols] = (
                (row - 128 * j == sub).astype(F32).astype(BF16)
            )

    loads[0].wait()
    loads[1].wait()
    x0 = nodes[0]
    tab[0, :N, :] = x0
    for k in range(4):
        one_hot(spread_column(sidx[0, k : k + 1, :]), N, o_x, k * HALO)
    fsrc[0] = mm(o_x[...], x0).astype(BF16)
    pl.semaphore_wait(barrier, D - 1 + G - 1)
    send_halo(0)

    for k in range(4):
        one_hot_t(sidx[0, k : k + 1, :], N, ot_x, k * HALO)
    for load in loads[2:5]:
        load.wait()
    sids = snd[...]
    past = sids - N
    edge_0 = cnt[0, 0]
    edge_1 = edge_0 + cnt[0, 1]
    edge_2 = edge_1 + cnt[0, 2]
    sids = (
        sids
        + jnp.where(past >= edge_0, HALO - cnt[0, 0], 0)
        + jnp.where(past >= edge_1, HALO - cnt[0, 1], 0)
        + jnp.where(past >= edge_2, HALO - cnt[0, 2], 0)
    )
    rids = rcv[...]
    for i in range(E // 256):
        part = slice(i * 256, (i + 1) * 256)
        one_hot(spread_column(rids[:, part]), N, o_r, i * 256)
        one_hot(spread_column(sids[:, part]), N + 4 * HALO, o_s, i * 256)
        one_hot_t(rids[:, part], N, ot_r, i * 256)
        one_hot_t(sids[:, part], N + 4 * HALO, ot_s, i * 256)

    for load in loads[5:]:
        load.wait()

    for l in range(L):
        def own_step(i, carry, l=l):
            rows = pl.ds(pl.multiple_of(i * C, C), C)
            e_rows = edges[0, rows, :] if l == 0 else e_in[l - 1, rows, :]
            sq[l, rows, :H] = mm(o_s[rows, :N], tab[l, :N, :]).astype(BF16)
            q_rows = mm(o_r[rows, :], tab[l, :N, :]).astype(BF16)
            sq[l, rows, H:] = q_rows
            slope[l, rows, :] = (
                mm(e_rows, w1[l, :H, :]) + mm(q_rows, w1[l, 2 * H :, :]) + bias[l, 0:1, :]
            )
            return carry

        lax.fori_loop(0, E // C, own_step, 0)
        wait_halo(l)

        def edge_step(i, carry, l=l):
            rows = pl.ds(pl.multiple_of(i * C, C), C)
            e_rows = edges[0, rows, :] if l == 0 else e_in[l - 1, rows, :]
            s_rows = sq[l, rows, :H] + mm(o_s[rows, N:], tab[l, N:, :]).astype(BF16)
            sq[l, rows, :H] = s_rows
            pre = slope[l, rows, :] + mm(s_rows, w1[l, H : 2 * H, :])
            h_rows, sl = silu_parts(pre)
            hid[l, rows, :] = h_rows
            slope[l, rows, :] = sl
            hat_rows, inv_rows = norm_parts(mm(h_rows, w2[l]) + bias[l, 1:2, :])
            hat[l, rows, :] = hat_rows
            inv[l, rows, :] = jnp.broadcast_to(inv_rows, hat_rows.shape)
            new = (e_rows.astype(F32) + hat_rows * gain[l, 0:1, :]).astype(BF16)
            if l + 1 < L:
                e_in[l, rows, :] = new
            else:
                e_last[rows, :] = new
            return carry

        lax.fori_loop(0, E // C, edge_step, 0)
        e_new = e_in[l] if l + 1 < L else e_last[...]
        x_rows = tab[l, :N, :]
        joined = jnp.concatenate([x_rows, mm(ot_r[...], e_new).astype(BF16)], axis=1)
        jn[l] = joined
        h_rows, sl = silu_parts(mm(joined, n1[l]) + bias[l, 2:3, :])
        nhid[l] = h_rows
        nslope[l] = sl
        hat_rows, inv_rows = norm_parts(mm(h_rows, n2[l]) + bias[l, 3:4, :])
        nhat[l] = hat_rows
        ninv[l] = jnp.broadcast_to(inv_rows, hat_rows.shape)
        x_new = (x_rows.astype(F32) + hat_rows * gain[l, 1:2, :]).astype(BF16)
        if l + 1 < L:
            tab[l + 1, :N, :] = x_new
            fsrc[l + 1] = mm(o_x[...], x_new).astype(BF16)
            send_halo(l + 1)
        else:
            x_out[0] = x_new

    for l in reversed(range(L)):
        cot = ncot[0].astype(F32) if l == L - 1 else x_cot.astype(F32)
        nh = nhat[l]
        dgn = fold(cot * nh)
        dmn = norm_back(cot, gain[l, 1:2, :], nh, ninv[l])
        dbn2 = fold(dmn)
        dmn = dmn.astype(BF16)
        dpn = mm_nt(dmn, n2[l]).astype(BF16).astype(F32) * nslope[l]
        dbn1 = fold(dpn)
        dpn = dpn.astype(BF16)
        djn = mm_nt(dpn, n1[l]).astype(BF16)
        dx[...] = cot + djn[:, :H].astype(F32)
        dab[...] = djn[:, H:]
        start_a(
            0,
            l,
            [mm(dpn.T, jn[l]).T, mm(dmn.T, nhid[l]).T]
            + [row_sum(v) for v in (dbn1, dbn2, dgn)],
        )
        if l + 1 < L:
            start_b(0, l + 1)

        def edge_back(i, carry, l=l):
            s_g, s_b2, s_b1 = carry
            rows = pl.ds(pl.multiple_of(i * C, C), C)
            c_rows = mm(o_r[rows, :], dab[...])
            if l < L - 1:
                c_rows = (de[rows, :].astype(F32) + c_rows).astype(BF16).astype(F32)
            hat_rows = hat[l, rows, :]
            dm_rows = norm_back(c_rows, gain[l, 0:1, :], hat_rows, inv[l, rows, :])
            s_g = s_g + fold(c_rows * hat_rows)
            s_b2 = s_b2 + fold(dm_rows)
            dm_b = dm_rows.astype(BF16)
            dm[rows, :] = dm_b
            dp_rows = mm_nt(dm_b, w2[l]).astype(BF16).astype(F32) * slope[l, rows, :]
            s_b1 = s_b1 + fold(dp_rows)
            dp_b = dp_rows.astype(BF16)
            dp[rows, :] = dp_b
            dj = mm_nt(dp_b, w1[l]).astype(BF16)
            back = (c_rows + dj[:, :H].astype(F32)).astype(BF16)
            if l == 0:
                e_grad[0, rows, :] = back
            else:
                de[rows, :] = back
            dsq[rows, :] = dj[:, H:]
            return s_g, s_b2, s_b1

        zero = jnp.zeros((8, H), F32)
        dge, dbe2, dbe1 = lax.fori_loop(0, E // C, edge_back, (zero, zero, zero))
        def halo_cots():
            bsrc[l] = mm(ot_s[N:, :], dsq[:, :H]).astype(BF16)
            send_ret(l)

        if l > 0:
            halo_cots()
        if l + 1 < L:
            start_b(1, l + 1)
        dp_t = dp[...].T
        e_rows = edges[0] if l == 0 else e_in[l - 1]
        start_a(
            1,
            l,
            [mm(dp_t, e_rows).T, mm(dp_t, sq[l]).T, mm(dm[...].T, hid[l]).T]
            + [row_sum(v) for v in (dbe1, dbe2, dge)],
        )
        if l == 0:
            halo_cots()
        total = dx[...] + mm(ot_s[:N, :], dsq[:, :H]) + mm(ot_r[...], dsq[:, H:])
        if l + 1 < L:
            start_c(0, l + 1)
        wait_ret(l)
        x_cot = (total + mm(ot_x[...], ret[l])).astype(BF16)
    x_grad[0] = x_cot

    start_b(0, 0)
    if L > 1:
        start_c(1, 1)
    start_b(1, 0)
    start_c(0, 0)
    start_c(1, 0)
    for l in reversed(range(L)):
        for t in range(2):
            end_c(t, l)

    for l in range(L):
        for k in range(4):
            @pl.when(out_ok[k])
            def _(k=k, l=l):
                fcopy(l, k).wait_send()

            @pl.when(in_ok[k])
            def _(k=k, l=l):
                bcopy(l, k).wait_send()
        for t in range(2):
            for off in range(1, D):
                a_copy(t, l, off).wait_send()
                c_copy(t, l, off).wait_send()
            for off in range(1, G):
                b_copy(t, l, off).wait_send()


def finish(scale, H, x0, xg0, eg0, sum_n, sum_e, x1, xg1, eg1, g_w1, g_w2, g_n1, g_n2, g_b, g_g):
    x1[...] = x0[...]
    xg1[...] = xg0[...]
    eg1[...] = eg0[...]
    L, D, share_n, _ = sum_n.shape
    share_e = sum_e.shape[2]
    for l in range(L):
        node = (sum_n[l].astype(F32) * scale).reshape(D * share_n, H)
        edge = (sum_e[l].astype(F32) * scale).reshape(D * share_e, H)
        g_n1[l] = node[: 2 * H]
        g_n2[l] = node[2 * H : 3 * H]
        g_w1[l] = edge[: 3 * H]
        g_w2[l] = edge[3 * H : 4 * H]
        node = node[3 * H : 3 * H + 8]
        edge = edge[4 * H : 4 * H + 8]
        g_b[l, 0:2, :] = edge[0:2]
        g_b[l, 2:4, :] = node[0:2]
        g_g[l, 0:1, :] = edge[2:3]
        g_g[l, 1:2, :] = node[2:3]


def shards(D, G, nodes, edges, node_cot, send_index, halo_count, senders, receivers, *weights):
    edge_in_w, edge_out_w, node_in_w, node_out_w, biases, gains = weights
    _, N, H = nodes.shape
    E = edges.shape[1]
    L = edge_in_w.shape[0]
    HALO = send_index.shape[2]
    C = 256
    share_n = -(-(3 * H + 3) // (8 * D)) * 8
    share_e = -(-(4 * H + 3) // (8 * D)) * 8
    dims = (D, G, L, N, E, H, HALO, C, share_n, share_e)
    T = N + 4 * HALO
    own_shape = (
        pltpu.VMEM(nodes.shape, BF16),
        pltpu.VMEM(nodes.shape, BF16),
        pltpu.VMEM(edges.shape, BF16),
        pltpu.VMEM((L, D, share_n, H), BF16),
        pltpu.VMEM((L, D, share_e, H), BF16),
    )
    out_shape = (
        jax.ShapeDtypeStruct(nodes.shape, BF16),
        jax.ShapeDtypeStruct(nodes.shape, BF16),
        jax.ShapeDtypeStruct(edges.shape, BF16),
        jax.ShapeDtypeStruct(edge_in_w.shape, F32),
        jax.ShapeDtypeStruct(edge_out_w.shape, F32),
        jax.ShapeDtypeStruct(node_in_w.shape, F32),
        jax.ShapeDtypeStruct(node_out_w.shape, F32),
        jax.ShapeDtypeStruct(biases.shape, F32),
        jax.ShapeDtypeStruct(gains.shape, F32),
    )
    V = pltpu.VMEM
    dma = pltpu.SemaphoreType.DMA
    scratch = [
        V((E, T), BF16),
        V((T, E), BF16),
        V((E, N), BF16),
        V((N, E), BF16),
        V((4 * HALO, N), BF16),
        V((N, 4 * HALO), BF16),
        V((L, T, H), BF16),
        V((max(L - 1, 1), E, H), BF16),
        V((E, H), BF16),
        V((L, E, 2 * H), BF16),
        V((L, E, H), BF16),
        V((L, E, H), F32),
        V((L, E, H), F32),
        V((L, E, H), F32),
        V((L, N, 2 * H), BF16),
        V((L, N, H), BF16),
        V((L, N, H), F32),
        V((L, N, H), F32),
        V((L, N, H), F32),
        V((E, H), BF16),
        V((E, H), BF16),
        V((E, H), BF16),
        V((E, 2 * H), BF16),
        V((N, H), F32),
        V((N, H), BF16),
        V((L, 4 * HALO, H), BF16),
        V((L, 4 * HALO, H), BF16),
        V((L, 4 * HALO, H), BF16),
        V((L, D, share_n, H), BF16),
        V((L, max(D - 1, 1), share_n, H), BF16),
        V((L, G, share_n, H), BF16),
        V((L, D, share_n, H), BF16),
        V((L, D, share_e, H), BF16),
        V((L, max(D - 1, 1), share_e, H), BF16),
        V((L, G, share_e, H), BF16),
        V((L, D, share_e, H), BF16),
        dma((L, 4)),
        dma((L, 4)),
        dma((L, 4)),
        dma((L, 4)),
        dma((2, L, D)),
        dma((2, L, D)),
        dma((2, L, G)),
        dma((2, L, G)),
        dma((2, L, D)),
        dma((2, L, D)),
        pltpu.SMEM(halo_count.shape, jnp.int32),
    ]
    operands = (nodes, edges, node_cot, send_index, senders, receivers) + weights
    scratch += [V(x.shape, x.dtype) for x in operands] + [dma((13,))]
    vm = pl.BlockSpec(memory_space=pltpu.VMEM)
    hbm = pl.BlockSpec(memory_space=pltpu.HBM)
    own = pl.pallas_call(
        functools.partial(kernel, dims),
        out_shape=own_shape,
        in_specs=[hbm] * 13,
        out_specs=tuple([vm] * 5),
        scratch_shapes=scratch,
        compiler_params=pltpu.CompilerParams(
            collective_id=0, has_side_effects=True, vmem_limit_bytes=VMEM_MAIN
        ),
    )(
        halo_count,
        *operands,
    )
    scale = (D * G * N) ** (-0.5)
    return pl.pallas_call(
        functools.partial(finish, scale, H),
        out_shape=out_shape,
        in_specs=[vm] * 5,
        out_specs=tuple([vm] * 9),
        compiler_params=pltpu.CompilerParams(vmem_limit_bytes=8 * 1024 * 1024),
    )(*own)


def solution(mesh):
    part3 = P(("dom", "group"), None, None)
    part2 = P(("dom", "group"), None)
    in_specs = (part3, part3, part3, part3, part2, part2, part2) + (P(),) * 6
    out_specs = (part3, part3, part3) + (P(),) * 6
    body = functools.partial(shards, mesh.shape["dom"], mesh.shape["group"])
    return jax.shard_map(
        body, mesh=mesh, in_specs=in_specs, out_specs=out_specs, check_vma=False
    )
```

```python
import functools

import jax
import jax.numpy as jnp
from jax import lax
from jax.experimental import pallas as pl
from jax.experimental.pallas import tpu as pltpu
from jax.sharding import PartitionSpec as P

F32 = jnp.float32
BF16 = jnp.bfloat16
MESH = pl.DeviceIdType.MESH
VMEM_MAIN = 58 * 1024 * 1024


def mm(a, b):
    return lax.dot_general(a, b, (((1,), (0,)), ((), ())), preferred_element_type=F32)


def mm_nt(a, b):
    return lax.dot_general(a, b, (((1,), (1,)), ((), ())), preferred_element_type=F32)


def fold(x):
    return jnp.sum(x.reshape(x.shape[0] // 8, 8, x.shape[1]), axis=0)


def row_sum(x):
    return jnp.sum(x, axis=0, keepdims=True)


def norm_parts(values):
    centre = values - jnp.mean(values, axis=-1, keepdims=True)
    spread = jnp.mean(centre * centre, axis=-1, keepdims=True)
    inv = lax.rsqrt(spread + 1e-05)
    return centre * inv, inv


def norm_back(cot, gain_row, hat, inv):
    u = cot * gain_row
    return inv * (
        u
        - jnp.mean(u, axis=-1, keepdims=True)
        - hat * jnp.mean(u * hat, axis=-1, keepdims=True)
    )


def silu_parts(pre):
    sig = 0.5 + 0.5 * jnp.tanh(0.5 * pre)
    return (pre * sig).astype(BF16), sig * (1.0 + pre * (1.0 - sig))


def kernel(
    dims,
    cnt_h,
    nodes_h,
    edges_h,
    ncot_h,
    sidx_h,
    snd_h,
    rcv_h,
    w1_h,
    w2_h,
    n1_h,
    n2_h,
    bias_h,
    gain_h,
    x_out,
    x_grad,
    e_grad,
    sum_n,
    sum_e,
    o_s,
    ot_s,
    o_r,
    ot_r,
    o_x,
    ot_x,
    tab,
    e_in,
    e_last,
    sq,
    hid,
    slope,
    hat,
    inv,
    jn,
    nhid,
    nslope,
    nhat,
    ninv,
    dm,
    dp,
    de,
    dsq,
    dx,
    dab,
    fsrc,
    bsrc,
    ret,
    grads_n,
    buf_an,
    buf_bn,
    grads_e,
    buf_ae,
    buf_be,
    fs,
    fr,
    bs,
    br,
    a_s,
    a_r,
    b_s,
    b_r,
    c_s,
    c_r,
    cnt,
    nodes,
    edges,
    ncot,
    sidx,
    snd,
    rcv,
    w1,
    w2,
    n1,
    n2,
    bias,
    gain,
    in_sem,
):
    D, G, L, N, E, H, HALO, C, share_n, share_e = dims
    shares = (share_n, share_e)
    grads = (grads_n, grads_e)
    buf_a = (buf_an, buf_ae)
    buf_b = (buf_bn, buf_be)
    gat = (sum_n, sum_e)
    loads = [
        pltpu.make_async_copy(src, dst, in_sem.at[i])
        for i, (src, dst) in enumerate(
            (
                (nodes_h, nodes),
                (sidx_h, sidx),
                (snd_h, snd),
                (rcv_h, rcv),
                (cnt_h, cnt),
                (edges_h, edges),
                (w1_h, w1),
                (w2_h, w2),
                (bias_h, bias),
                (gain_h, gain),
                (n1_h, n1),
                (n2_h, n2),
                (ncot_h, ncot),
            )
        )
    ]
    for load in loads:
        load.start()
    d = lax.axis_index("dom")
    g = lax.axis_index("group")

    has_up = d + 1 < D
    has_down = d > 0
    has_right = g + 1 < G
    has_left = g > 0
    out_ok = (has_up, has_down, has_right, has_left)
    in_ok = (has_down, has_up, has_left, has_right)
    out_dev = ({"dom": d + 1}, {"dom": d - 1}, {"group": g + 1}, {"group": g - 1})
    in_dev = ({"dom": d - 1}, {"dom": d + 1}, {"group": g - 1}, {"group": g + 1})

    def fcopy(l, k):
        return pltpu.make_async_remote_copy(
            src_ref=fsrc.at[l, pl.ds(k * HALO, HALO)],
            dst_ref=tab.at[l, pl.ds(N + k * HALO, HALO)],
            send_sem=fs.at[l, k],
            recv_sem=fr.at[l, k],
            device_id=out_dev[k],
            device_id_type=MESH,
        )

    def bcopy(l, k):
        return pltpu.make_async_remote_copy(
            src_ref=bsrc.at[l, pl.ds(k * HALO, HALO)],
            dst_ref=ret.at[l, pl.ds(k * HALO, HALO)],
            send_sem=bs.at[l, k],
            recv_sem=br.at[l, k],
            device_id=in_dev[k],
            device_id_type=MESH,
        )

    def send_halo(l):
        for k in range(4):
            @pl.when(out_ok[k])
            def _(k=k):
                fcopy(l, k).start()

    def wait_halo(l):
        for k in range(4):
            @pl.when(in_ok[k])
            def _(k=k):
                fcopy(l, k).wait_recv()

    def send_ret(l):
        for k in range(4):
            @pl.when(in_ok[k])
            def _(k=k):
                bcopy(l, k).start()

    def wait_ret(l):
        for k in range(4):
            @pl.when(out_ok[k])
            def _(k=k):
                bcopy(l, k).wait_recv()

    def a_copy(t, l, off):
        peer = lax.rem(d + off, D)
        return pltpu.make_async_remote_copy(
            src_ref=grads[t].at[l, peer],
            dst_ref=buf_a[t].at[l, off - 1],
            send_sem=a_s.at[t, l, off - 1],
            recv_sem=a_r.at[t, l, off - 1],
            device_id={"dom": peer},
            device_id_type=MESH,
        )

    def b_copy(t, l, off):
        return pltpu.make_async_remote_copy(
            src_ref=buf_b[t].at[l, g],
            dst_ref=buf_b[t].at[l, g],
            send_sem=b_s.at[t, l, off - 1],
            recv_sem=b_r.at[t, l, off - 1],
            device_id={"group": lax.rem(g + off, G)},
            device_id_type=MESH,
        )

    def c_copy(t, l, off):
        return pltpu.make_async_remote_copy(
            src_ref=gat[t].at[l, d],
            dst_ref=gat[t].at[l, d],
            send_sem=c_s.at[t, l, off - 1],
            recv_sem=c_r.at[t, l, off - 1],
            device_id={"dom": lax.rem(d + off, D)},
            device_id_type=MESH,
        )

    def start_a(t, l, pieces):
        rows = sum(p.shape[0] for p in pieces)
        pad = jnp.zeros((D * shares[t] - rows, H), F32)
        whole = jnp.concatenate(list(pieces) + [pad], axis=0)
        grads[t][l] = whole.reshape(D, shares[t], H).astype(BF16)
        for off in range(1, D):
            a_copy(t, l, off).start()

    def start_b(t, l):
        acc = grads[t][l, d].astype(F32)
        for off in range(1, D):
            a_copy(t, l, off).wait_recv()
            acc = acc + buf_a[t][l, off - 1].astype(F32)
        buf_b[t][l, g] = acc.astype(BF16)
        for off in range(1, G):
            b_copy(t, l, off).start()

    def start_c(t, l):
        for off in range(1, G):
            b_copy(t, l, off).wait_recv()
        acc = buf_b[t][l, 0].astype(F32)
        for i in range(1, G):
            acc = acc + buf_b[t][l, i].astype(F32)
        gat[t][l, d] = acc.astype(BF16)
        for off in range(1, D):
            c_copy(t, l, off).start()

    def end_c(t, l):
        for off in range(1, D):
            c_copy(t, l, off).wait_recv()

    for l in range(L):
        tab[l, N:, :] = jnp.zeros((4 * HALO, H), BF16)
        ret[l] = jnp.zeros((4 * HALO, H), BF16)
    barrier = pltpu.get_barrier_semaphore()
    for off in range(1, D):
        pl.semaphore_signal(
            barrier, inc=1, device_id={"dom": lax.rem(d + off, D)}, device_id_type=MESH
        )
    for off in range(1, G):
        pl.semaphore_signal(
            barrier, inc=1, device_id={"group": lax.rem(g + off, G)}, device_id_type=MESH
        )

    def spread_column(row):
        return jnp.broadcast_to(row, (128, row.shape[1])).T

    def one_hot(column, width, ref, row0):
        rows = column.shape[0]
        lane = lax.broadcasted_iota(jnp.int32, (rows, 128), 1)
        for j in range(width // 128):
            ref[row0 : row0 + rows, j * 128 : (j + 1) * 128] = (
                (column - 128 * j == lane).astype(F32).astype(BF16)
            )

    def one_hot_t(row, height, ref, col0):
        cols = row.shape[1]
        sub = lax.broadcasted_iota(jnp.int32, (128, cols), 0)
        for j in range(height // 128):
            ref[j * 128 : (j + 1) * 128, col0 : col0 + cols] = (
                (row - 128 * j == sub).astype(F32).astype(BF16)
            )

    loads[0].wait()
    loads[1].wait()
    x0 = nodes[0]
    tab[0, :N, :] = x0
    for k in range(4):
        one_hot(spread_column(sidx[0, k : k + 1, :]), N, o_x, k * HALO)
    fsrc[0] = mm(o_x[...], x0).astype(BF16)
    pl.semaphore_wait(barrier, D - 1 + G - 1)
    send_halo(0)

    for load in loads[2:5]:
        load.wait()
    sids = snd[...]
    past = sids - N
    edge_0 = cnt[0, 0]
    edge_1 = edge_0 + cnt[0, 1]
    edge_2 = edge_1 + cnt[0, 2]
    sids = (
        sids
        + jnp.where(past >= edge_0, HALO - cnt[0, 0], 0)
        + jnp.where(past >= edge_1, HALO - cnt[0, 1], 0)
        + jnp.where(past >= edge_2, HALO - cnt[0, 2], 0)
    )
    rids = rcv[...]
    for i in range(E // 256):
        part = slice(i * 256, (i + 1) * 256)
        one_hot(spread_column(rids[:, part]), N, o_r, i * 256)
        one_hot(spread_column(sids[:, part]), N + 4 * HALO, o_s, i * 256)
        one_hot_t(rids[:, part], N, ot_r, i * 256)

    for load in loads[5:]:
        load.wait()

    for l in range(L):
        def own_step(i, carry, l=l):
            rows = pl.ds(pl.multiple_of(i * C, C), C)
            e_rows = edges[0, rows, :] if l == 0 else e_in[l - 1, rows, :]
            sq[l, rows, :H] = mm(o_s[rows, :N], tab[l, :N, :]).astype(BF16)
            q_rows = mm(o_r[rows, :], tab[l, :N, :]).astype(BF16)
            sq[l, rows, H:] = q_rows
            slope[l, rows, :] = (
                mm(e_rows, w1[l, :H, :]) + mm(q_rows, w1[l, 2 * H :, :]) + bias[l, 0:1, :]
            )
            return carry

        lax.fori_loop(0, E // C, own_step, 0)
        if l == L - 1:
            for k in range(4):
                one_hot_t(sidx[0, k : k + 1, :], N, ot_x, k * HALO)
            for i in range(E // 256):
                part = slice(i * 256, (i + 1) * 256)
                one_hot_t(sids[:, part], N + 4 * HALO, ot_s, i * 256)
        wait_halo(l)

        def edge_step(i, carry, l=l):
            rows = pl.ds(pl.multiple_of(i * C, C), C)
            e_rows = edges[0, rows, :] if l == 0 else e_in[l - 1, rows, :]
            s_rows = sq[l, rows, :H] + mm(o_s[rows, N:], tab[l, N:, :]).astype(BF16)
            sq[l, rows, :H] = s_rows
            pre = slope[l, rows, :] + mm(s_rows, w1[l, H : 2 * H, :])
            h_rows, sl = silu_parts(pre)
            hid[l, rows, :] = h_rows
            slope[l, rows, :] = sl
            hat_rows, inv_rows = norm_parts(mm(h_rows, w2[l]) + bias[l, 1:2, :])
            hat[l, rows, :] = hat_rows
            inv[l, rows, :] = jnp.broadcast_to(inv_rows, hat_rows.shape)
            new = (e_rows.astype(F32) + hat_rows * gain[l, 0:1, :]).astype(BF16)
            if l + 1 < L:
                e_in[l, rows, :] = new
            else:
                e_last[rows, :] = new
            return carry

        lax.fori_loop(0, E // C, edge_step, 0)
        e_new = e_in[l] if l + 1 < L else e_last[...]
        x_rows = tab[l, :N, :]
        joined = jnp.concatenate([x_rows, mm(ot_r[...], e_new).astype(BF16)], axis=1)
        jn[l] = joined
        h_rows, sl = silu_parts(mm(joined, n1[l]) + bias[l, 2:3, :])
        nhid[l] = h_rows
        nslope[l] = sl
        hat_rows, inv_rows = norm_parts(mm(h_rows, n2[l]) + bias[l, 3:4, :])
        nhat[l] = hat_rows
        ninv[l] = jnp.broadcast_to(inv_rows, hat_rows.shape)
        x_new = (x_rows.astype(F32) + hat_rows * gain[l, 1:2, :]).astype(BF16)
        if l + 1 < L:
            tab[l + 1, :N, :] = x_new
            fsrc[l + 1] = mm(o_x[...], x_new).astype(BF16)
            send_halo(l + 1)
        else:
            x_out[0] = x_new

    for l in reversed(range(L)):
        cot = ncot[0].astype(F32) if l == L - 1 else x_cot.astype(F32)
        nh = nhat[l]
        dgn = fold(cot * nh)
        dmn = norm_back(cot, gain[l, 1:2, :], nh, ninv[l])
        dbn2 = fold(dmn)
        dmn = dmn.astype(BF16)
        dpn = mm_nt(dmn, n2[l]).astype(BF16).astype(F32) * nslope[l]
        dbn1 = fold(dpn)
        dpn = dpn.astype(BF16)
        djn = mm_nt(dpn, n1[l]).astype(BF16)
        dx[...] = cot + djn[:, :H].astype(F32)
        dab[...] = djn[:, H:]
        start_a(
            0,
            l,
            [mm(dpn.T, jn[l]).T, mm(dmn.T, nhid[l]).T]
            + [row_sum(v) for v in (dbn1, dbn2, dgn)],
        )
        if l + 1 < L:
            start_b(0, l + 1)

        def edge_back(i, carry, l=l):
            s_g, s_b2, s_b1 = carry
            rows = pl.ds(pl.multiple_of(i * C, C), C)
            c_rows = mm(o_r[rows, :], dab[...])
            if l < L - 1:
                c_rows = (de[rows, :].astype(F32) + c_rows).astype(BF16).astype(F32)
            hat_rows = hat[l, rows, :]
            dm_rows = norm_back(c_rows, gain[l, 0:1, :], hat_rows, inv[l, rows, :])
            s_g = s_g + fold(c_rows * hat_rows)
            s_b2 = s_b2 + fold(dm_rows)
            dm_b = dm_rows.astype(BF16)
            dm[rows, :] = dm_b
            dp_rows = mm_nt(dm_b, w2[l]).astype(BF16).astype(F32) * slope[l, rows, :]
            s_b1 = s_b1 + fold(dp_rows)
            dp_b = dp_rows.astype(BF16)
            dp[rows, :] = dp_b
            dj = mm_nt(dp_b, w1[l]).astype(BF16)
            back = (c_rows + dj[:, :H].astype(F32)).astype(BF16)
            if l == 0:
                e_grad[0, rows, :] = back
            else:
                de[rows, :] = back
            dsq[rows, :] = dj[:, H:]
            return s_g, s_b2, s_b1

        zero = jnp.zeros((8, H), F32)
        dge, dbe2, dbe1 = lax.fori_loop(0, E // C, edge_back, (zero, zero, zero))
        def halo_cots():
            bsrc[l] = mm(ot_s[N:, :], dsq[:, :H]).astype(BF16)
            send_ret(l)

        if l > 0:
            halo_cots()
        if l + 1 < L:
            start_b(1, l + 1)
        dp_t = dp[...].T
        e_rows = edges[0] if l == 0 else e_in[l - 1]
        start_a(
            1,
            l,
            [mm(dp_t, e_rows).T, mm(dp_t, sq[l]).T, mm(dm[...].T, hid[l]).T]
            + [row_sum(v) for v in (dbe1, dbe2, dge)],
        )
        if l == 0:
            start_b(0, 0)
            halo_cots()
        if l + 1 < L:
            start_c(0, l + 1)
            start_c(1, l + 1)
        total = dx[...] + mm(ot_s[:N, :], dsq[:, :H]) + mm(ot_r[...], dsq[:, H:])
        wait_ret(l)
        x_cot = (total + mm(ot_x[...], ret[l])).astype(BF16)
    x_grad[0] = x_cot

    start_c(0, 0)
    start_b(1, 0)
    start_c(1, 0)
    for l in reversed(range(L)):
        for t in range(2):
            end_c(t, l)

    for l in range(L):
        for k in range(4):
            @pl.when(out_ok[k])
            def _(k=k, l=l):
                fcopy(l, k).wait_send()

            @pl.when(in_ok[k])
            def _(k=k, l=l):
                bcopy(l, k).wait_send()
        for t in range(2):
            for off in range(1, D):
                a_copy(t, l, off).wait_send()
                c_copy(t, l, off).wait_send()
            for off in range(1, G):
                b_copy(t, l, off).wait_send()


def finish(scale, H, x0, xg0, eg0, sum_n, sum_e, x1, xg1, eg1, g_w1, g_w2, g_n1, g_n2, g_b, g_g):
    x1[...] = x0[...]
    xg1[...] = xg0[...]
    eg1[...] = eg0[...]
    L, D, share_n, _ = sum_n.shape
    share_e = sum_e.shape[2]
    for l in range(L):
        node = (sum_n[l].astype(F32) * scale).reshape(D * share_n, H)
        edge = (sum_e[l].astype(F32) * scale).reshape(D * share_e, H)
        g_n1[l] = node[: 2 * H]
        g_n2[l] = node[2 * H : 3 * H]
        g_w1[l] = edge[: 3 * H]
        g_w2[l] = edge[3 * H : 4 * H]
        node = node[3 * H : 3 * H + 8]
        edge = edge[4 * H : 4 * H + 8]
        g_b[l, 0:2, :] = edge[0:2]
        g_b[l, 2:4, :] = node[0:2]
        g_g[l, 0:1, :] = edge[2:3]
        g_g[l, 1:2, :] = node[2:3]


def shards(D, G, nodes, edges, node_cot, send_index, halo_count, senders, receivers, *weights):
    edge_in_w, edge_out_w, node_in_w, node_out_w, biases, gains = weights
    _, N, H = nodes.shape
    E = edges.shape[1]
    L = edge_in_w.shape[0]
    HALO = send_index.shape[2]
    C = 512
    share_n = -(-(3 * H + 3) // (8 * D)) * 8
    share_e = -(-(4 * H + 3) // (8 * D)) * 8
    dims = (D, G, L, N, E, H, HALO, C, share_n, share_e)
    T = N + 4 * HALO
    own_shape = (
        pltpu.VMEM(nodes.shape, BF16),
        pltpu.VMEM(nodes.shape, BF16),
        pltpu.VMEM(edges.shape, BF16),
        pltpu.VMEM((L, D, share_n, H), BF16),
        pltpu.VMEM((L, D, share_e, H), BF16),
    )
    out_shape = (
        jax.ShapeDtypeStruct(nodes.shape, BF16),
        jax.ShapeDtypeStruct(nodes.shape, BF16),
        jax.ShapeDtypeStruct(edges.shape, BF16),
        jax.ShapeDtypeStruct(edge_in_w.shape, F32),
        jax.ShapeDtypeStruct(edge_out_w.shape, F32),
        jax.ShapeDtypeStruct(node_in_w.shape, F32),
        jax.ShapeDtypeStruct(node_out_w.shape, F32),
        jax.ShapeDtypeStruct(biases.shape, F32),
        jax.ShapeDtypeStruct(gains.shape, F32),
    )
    V = pltpu.VMEM
    dma = pltpu.SemaphoreType.DMA
    scratch = [
        V((E, T), BF16),
        V((T, E), BF16),
        V((E, N), BF16),
        V((N, E), BF16),
        V((4 * HALO, N), BF16),
        V((N, 4 * HALO), BF16),
        V((L, T, H), BF16),
        V((max(L - 1, 1), E, H), BF16),
        V((E, H), BF16),
        V((L, E, 2 * H), BF16),
        V((L, E, H), BF16),
        V((L, E, H), F32),
        V((L, E, H), F32),
        V((L, E, H), F32),
        V((L, N, 2 * H), BF16),
        V((L, N, H), BF16),
        V((L, N, H), F32),
        V((L, N, H), F32),
        V((L, N, H), F32),
        V((E, H), BF16),
        V((E, H), BF16),
        V((E, H), BF16),
        V((E, 2 * H), BF16),
        V((N, H), F32),
        V((N, H), BF16),
        V((L, 4 * HALO, H), BF16),
        V((L, 4 * HALO, H), BF16),
        V((L, 4 * HALO, H), BF16),
        V((L, D, share_n, H), BF16),
        V((L, max(D - 1, 1), share_n, H), BF16),
        V((L, G, share_n, H), BF16),
        V((L, D, share_e, H), BF16),
        V((L, max(D - 1, 1), share_e, H), BF16),
        V((L, G, share_e, H), BF16),
        dma((L, 4)),
        dma((L, 4)),
        dma((L, 4)),
        dma((L, 4)),
        dma((2, L, D)),
        dma((2, L, D)),
        dma((2, L, G)),
        dma((2, L, G)),
        dma((2, L, D)),
        dma((2, L, D)),
        pltpu.SMEM(halo_count.shape, jnp.int32),
    ]
    operands = (nodes, edges, node_cot, send_index, senders, receivers) + weights
    scratch += [V(x.shape, x.dtype) for x in operands] + [dma((13,))]
    vm = pl.BlockSpec(memory_space=pltpu.VMEM)
    hbm = pl.BlockSpec(memory_space=pltpu.HBM)
    own = pl.pallas_call(
        functools.partial(kernel, dims),
        out_shape=own_shape,
        in_specs=[hbm] * 13,
        out_specs=tuple([vm] * 5),
        scratch_shapes=scratch,
        compiler_params=pltpu.CompilerParams(
            collective_id=0, has_side_effects=True, vmem_limit_bytes=VMEM_MAIN
        ),
    )(
        halo_count,
        *operands,
    )
    scale = (D * G * N) ** (-0.5)
    return pl.pallas_call(
        functools.partial(finish, scale, H),
        out_shape=out_shape,
        in_specs=[vm] * 5,
        out_specs=tuple([vm] * 9),
        compiler_params=pltpu.CompilerParams(vmem_limit_bytes=8 * 1024 * 1024),
    )(*own)


def solution(mesh):
    part3 = P(("dom", "group"), None, None)
    part2 = P(("dom", "group"), None)
    in_specs = (part3, part3, part3, part3, part2, part2, part2) + (P(),) * 6
    out_specs = (part3, part3, part3) + (P(),) * 6
    body = functools.partial(shards, mesh.shape["dom"], mesh.shape["group"])
    return jax.shard_map(
        body, mesh=mesh, in_specs=in_specs, out_specs=out_specs, check_vma=False
    )
```

```python
import functools

import jax
import jax.numpy as jnp
from jax import lax
from jax.experimental import pallas as pl
from jax.experimental.pallas import tpu as pltpu
from jax.sharding import PartitionSpec as P

F32 = jnp.float32
BF16 = jnp.bfloat16
MESH = pl.DeviceIdType.MESH
VMEM_MAIN = 58 * 1024 * 1024


def mm(a, b):
    return lax.dot_general(a, b, (((1,), (0,)), ((), ())), preferred_element_type=F32)


def mm_nt(a, b):
    return lax.dot_general(a, b, (((1,), (1,)), ((), ())), preferred_element_type=F32)


def fold(x):
    return jnp.sum(x.reshape(x.shape[0] // 8, 8, x.shape[1]), axis=0)


def row_sum(x):
    return jnp.sum(x, axis=0, keepdims=True)


def norm_parts(values):
    centre = values - jnp.mean(values, axis=-1, keepdims=True)
    spread = jnp.mean(centre * centre, axis=-1, keepdims=True)
    inv = lax.rsqrt(spread + 1e-05)
    return centre * inv, inv


def norm_back(cot, gain_row, hat, inv):
    u = cot * gain_row
    return inv * (
        u
        - jnp.mean(u, axis=-1, keepdims=True)
        - hat * jnp.mean(u * hat, axis=-1, keepdims=True)
    )


def silu_parts(pre):
    sig = 0.5 + 0.5 * jnp.tanh(0.5 * pre)
    return (pre * sig).astype(BF16), sig * (1.0 + pre * (1.0 - sig))


def kernel(
    dims,
    cnt_h,
    nodes_h,
    edges_h,
    ncot_h,
    sidx_h,
    snd_h,
    rcv_h,
    w1_h,
    w2_h,
    n1_h,
    n2_h,
    bias_h,
    gain_h,
    x_out,
    x_grad,
    e_grad,
    sum_n,
    sum_e,
    o_s,
    ot_s,
    o_r,
    ot_r,
    o_x,
    ot_x,
    tab,
    e_in,
    e_last,
    sq,
    hid,
    slope,
    hat,
    inv,
    jn,
    nhid,
    nslope,
    nhat,
    ninv,
    dm,
    dp,
    de,
    dsq,
    dx,
    dab,
    fsrc,
    bsrc,
    ret,
    grads_n,
    buf_an,
    buf_bn,
    grads_e,
    buf_ae,
    buf_be,
    fs,
    fr,
    bs,
    br,
    a_s,
    a_r,
    b_s,
    b_r,
    c_s,
    c_r,
    cnt,
    nodes,
    edges,
    ncot,
    sidx,
    snd,
    rcv,
    w1,
    w2,
    n1,
    n2,
    bias,
    gain,
    in_sem,
):
    D, G, L, N, E, H, HALO, C, share_n, share_e = dims
    shares = (share_n, share_e)
    grads = (grads_n, grads_e)
    buf_a = (buf_an, buf_ae)
    buf_b = (buf_bn, buf_be)
    gat = (sum_n, sum_e)
    loads = [
        pltpu.make_async_copy(src, dst, in_sem.at[i])
        for i, (src, dst) in enumerate(
            (
                (nodes_h, nodes),
                (sidx_h, sidx),
                (snd_h, snd),
                (rcv_h, rcv),
                (cnt_h, cnt),
                (edges_h, edges),
                (w1_h, w1),
                (w2_h, w2),
                (bias_h, bias),
                (gain_h, gain),
                (n1_h, n1),
                (n2_h, n2),
                (ncot_h, ncot),
            )
        )
    ]
    for load in loads:
        load.start()
    d = lax.axis_index("dom")
    g = lax.axis_index("group")

    has_up = d + 1 < D
    has_down = d > 0
    has_right = g + 1 < G
    has_left = g > 0
    out_ok = (has_up, has_down, has_right, has_left)
    in_ok = (has_down, has_up, has_left, has_right)
    out_dev = ({"dom": d + 1}, {"dom": d - 1}, {"group": g + 1}, {"group": g - 1})
    in_dev = ({"dom": d - 1}, {"dom": d + 1}, {"group": g - 1}, {"group": g + 1})

    def fcopy(l, k):
        return pltpu.make_async_remote_copy(
            src_ref=fsrc.at[l, pl.ds(k * HALO, HALO)],
            dst_ref=tab.at[l, pl.ds(N + k * HALO, HALO)],
            send_sem=fs.at[l, k],
            recv_sem=fr.at[l, k],
            device_id=out_dev[k],
            device_id_type=MESH,
        )

    def bcopy(l, k):
        return pltpu.make_async_remote_copy(
            src_ref=bsrc.at[l, pl.ds(k * HALO, HALO)],
            dst_ref=ret.at[l, pl.ds(k * HALO, HALO)],
            send_sem=bs.at[l, k],
            recv_sem=br.at[l, k],
            device_id=in_dev[k],
            device_id_type=MESH,
        )

    def send_halo(l):
        for k in range(4):
            @pl.when(out_ok[k])
            def _(k=k):
                fcopy(l, k).start()

    def wait_halo(l):
        for k in range(4):
            @pl.when(in_ok[k])
            def _(k=k):
                fcopy(l, k).wait_recv()

    def send_ret(l):
        for k in range(4):
            @pl.when(in_ok[k])
            def _(k=k):
                bcopy(l, k).start()

    def wait_ret(l):
        for k in range(4):
            @pl.when(out_ok[k])
            def _(k=k):
                bcopy(l, k).wait_recv()

    def a_copy(t, l, off):
        peer = lax.rem(d + off, D)
        return pltpu.make_async_remote_copy(
            src_ref=grads[t].at[l, peer],
            dst_ref=buf_a[t].at[l, off - 1],
            send_sem=a_s.at[t, l, off - 1],
            recv_sem=a_r.at[t, l, off - 1],
            device_id={"dom": peer},
            device_id_type=MESH,
        )

    def b_copy(t, l, off):
        return pltpu.make_async_remote_copy(
            src_ref=buf_b[t].at[l, g],
            dst_ref=buf_b[t].at[l, g],
            send_sem=b_s.at[t, l, off - 1],
            recv_sem=b_r.at[t, l, off - 1],
            device_id={"group": lax.rem(g + off, G)},
            device_id_type=MESH,
        )

    def c_copy(t, l, off):
        return pltpu.make_async_remote_copy(
            src_ref=gat[t].at[l, d],
            dst_ref=gat[t].at[l, d],
            send_sem=c_s.at[t, l, off - 1],
            recv_sem=c_r.at[t, l, off - 1],
            device_id={"dom": lax.rem(d + off, D)},
            device_id_type=MESH,
        )

    def start_a(t, l, pieces):
        rows = sum(p.shape[0] for p in pieces)
        pad = jnp.zeros((D * shares[t] - rows, H), F32)
        whole = jnp.concatenate(list(pieces) + [pad], axis=0)
        grads[t][l] = whole.reshape(D, shares[t], H).astype(BF16)
        for off in range(1, D):
            a_copy(t, l, off).start()

    def start_b(t, l):
        acc = grads[t][l, d].astype(F32)
        for off in range(1, D):
            a_copy(t, l, off).wait_recv()
            acc = acc + buf_a[t][l, off - 1].astype(F32)
        buf_b[t][l, g] = acc.astype(BF16)
        for off in range(1, G):
            b_copy(t, l, off).start()

    def start_c(t, l):
        for off in range(1, G):
            b_copy(t, l, off).wait_recv()
        acc = buf_b[t][l, 0].astype(F32)
        for i in range(1, G):
            acc = acc + buf_b[t][l, i].astype(F32)
        gat[t][l, d] = acc.astype(BF16)
        for off in range(1, D):
            c_copy(t, l, off).start()

    def end_c(t, l):
        for off in range(1, D):
            c_copy(t, l, off).wait_recv()

    for l in range(L):
        tab[l, N:, :] = jnp.zeros((4 * HALO, H), BF16)
        ret[l] = jnp.zeros((4 * HALO, H), BF16)
    barrier = pltpu.get_barrier_semaphore()
    for off in range(1, D):
        pl.semaphore_signal(
            barrier, inc=1, device_id={"dom": lax.rem(d + off, D)}, device_id_type=MESH
        )
    for off in range(1, G):
        pl.semaphore_signal(
            barrier, inc=1, device_id={"group": lax.rem(g + off, G)}, device_id_type=MESH
        )

    def spread_column(row):
        return jnp.broadcast_to(row, (128, row.shape[1])).T

    def one_hot(column, width, ref, row0):
        rows = column.shape[0]
        lane = lax.broadcasted_iota(jnp.int32, (rows, 128), 1)
        for j in range(width // 128):
            ref[row0 : row0 + rows, j * 128 : (j + 1) * 128] = (
                (column - 128 * j == lane).astype(F32).astype(BF16)
            )

    def one_hot_t(row, height, ref, col0):
        cols = row.shape[1]
        sub = lax.broadcasted_iota(jnp.int32, (128, cols), 0)
        for j in range(height // 128):
            ref[j * 128 : (j + 1) * 128, col0 : col0 + cols] = (
                (row - 128 * j == sub).astype(F32).astype(BF16)
            )

    loads[0].wait()
    loads[1].wait()
    x0 = nodes[0]
    tab[0, :N, :] = x0
    for k in range(4):
        one_hot(spread_column(sidx[0, k : k + 1, :]), N, o_x, k * HALO)
    fsrc[0] = mm(o_x[...], x0).astype(BF16)
    pl.semaphore_wait(barrier, D - 1 + G - 1)
    send_halo(0)

    for load in loads[2:5]:
        load.wait()
    sids = snd[...]
    past = sids - N
    edge_0 = cnt[0, 0]
    edge_1 = edge_0 + cnt[0, 1]
    edge_2 = edge_1 + cnt[0, 2]
    sids = (
        sids
        + jnp.where(past >= edge_0, HALO - cnt[0, 0], 0)
        + jnp.where(past >= edge_1, HALO - cnt[0, 1], 0)
        + jnp.where(past >= edge_2, HALO - cnt[0, 2], 0)
    )
    rids = rcv[...]
    for i in range(E // 256):
        part = slice(i * 256, (i + 1) * 256)
        one_hot(spread_column(rids[:, part]), N, o_r, i * 256)
        one_hot(spread_column(sids[:, part]), N + 4 * HALO, o_s, i * 256)
        one_hot_t(rids[:, part], N, ot_r, i * 256)

    for load in loads[5:]:
        load.wait()

    for l in range(L):
        def own_step(i, carry, l=l):
            rows = pl.ds(pl.multiple_of(i * C, C), C)
            e_rows = edges[0, rows, :] if l == 0 else e_in[l - 1, rows, :]
            sq[l, rows, :H] = mm(o_s[rows, :N], tab[l, :N, :]).astype(BF16)
            q_rows = mm(o_r[rows, :], tab[l, :N, :]).astype(BF16)
            sq[l, rows, H:] = q_rows
            slope[l, rows, :] = (
                mm(e_rows, w1[l, :H, :]) + mm(q_rows, w1[l, 2 * H :, :]) + bias[l, 0:1, :]
            )
            return carry

        lax.fori_loop(0, E // C, own_step, 0)
        if l == L - 1:
            for k in range(4):
                one_hot_t(sidx[0, k : k + 1, :], N, ot_x, k * HALO)
            for i in range(E // 256):
                part = slice(i * 256, (i + 1) * 256)
                one_hot_t(sids[:, part], N + 4 * HALO, ot_s, i * 256)
        wait_halo(l)

        def edge_step(i, carry, l=l):
            rows = pl.ds(pl.multiple_of(i * C, C), C)
            e_rows = edges[0, rows, :] if l == 0 else e_in[l - 1, rows, :]
            s_rows = sq[l, rows, :H] + mm(o_s[rows, N:], tab[l, N:, :]).astype(BF16)
            sq[l, rows, :H] = s_rows
            pre = slope[l, rows, :] + mm(s_rows, w1[l, H : 2 * H, :])
            h_rows, sl = silu_parts(pre)
            hid[l, rows, :] = h_rows
            slope[l, rows, :] = sl
            hat_rows, inv_rows = norm_parts(mm(h_rows, w2[l]) + bias[l, 1:2, :])
            hat[l, rows, :] = hat_rows
            inv[l, rows, :] = jnp.broadcast_to(inv_rows, hat_rows.shape)
            new = (e_rows.astype(F32) + hat_rows * gain[l, 0:1, :]).astype(BF16)
            if l + 1 < L:
                e_in[l, rows, :] = new
            else:
                e_last[rows, :] = new
            return carry

        lax.fori_loop(0, E // C, edge_step, 0)
        e_new = e_in[l] if l + 1 < L else e_last[...]
        x_rows = tab[l, :N, :]
        joined = jnp.concatenate([x_rows, mm(ot_r[...], e_new).astype(BF16)], axis=1)
        jn[l] = joined
        h_rows, sl = silu_parts(mm(joined, n1[l]) + bias[l, 2:3, :])
        nhid[l] = h_rows
        nslope[l] = sl
        hat_rows, inv_rows = norm_parts(mm(h_rows, n2[l]) + bias[l, 3:4, :])
        nhat[l] = hat_rows
        ninv[l] = jnp.broadcast_to(inv_rows, hat_rows.shape)
        x_new = (x_rows.astype(F32) + hat_rows * gain[l, 1:2, :]).astype(BF16)
        if l + 1 < L:
            tab[l + 1, :N, :] = x_new
            fsrc[l + 1] = mm(o_x[...], x_new).astype(BF16)
            send_halo(l + 1)
        else:
            x_out[0] = x_new

    for l in reversed(range(L)):
        cot = ncot[0].astype(F32) if l == L - 1 else x_cot.astype(F32)
        nh = nhat[l]
        dgn = fold(cot * nh)
        dmn = norm_back(cot, gain[l, 1:2, :], nh, ninv[l])
        dbn2 = fold(dmn)
        dmn = dmn.astype(BF16)
        dpn = mm_nt(dmn, n2[l]).astype(BF16).astype(F32) * nslope[l]
        dbn1 = fold(dpn)
        dpn = dpn.astype(BF16)
        djn = mm_nt(dpn, n1[l]).astype(BF16)
        dx[...] = cot + djn[:, :H].astype(F32)
        dab[...] = djn[:, H:]
        start_a(
            0,
            l,
            [mm(dpn.T, jn[l]).T, mm(dmn.T, nhid[l]).T]
            + [row_sum(v) for v in (dbn1, dbn2, dgn)],
        )
        if l + 1 < L:
            start_b(0, l + 1)

        def edge_back(i, carry, l=l):
            s_g, s_b2, s_b1 = carry
            rows = pl.ds(pl.multiple_of(i * C, C), C)
            c_rows = mm(o_r[rows, :], dab[...])
            if l < L - 1:
                c_rows = (de[rows, :].astype(F32) + c_rows).astype(BF16).astype(F32)
            hat_rows = hat[l, rows, :]
            dm_rows = norm_back(c_rows, gain[l, 0:1, :], hat_rows, inv[l, rows, :])
            s_g = s_g + fold(c_rows * hat_rows)
            s_b2 = s_b2 + fold(dm_rows)
            dm_b = dm_rows.astype(BF16)
            dm[rows, :] = dm_b
            dp_rows = mm_nt(dm_b, w2[l]).astype(BF16).astype(F32) * slope[l, rows, :]
            s_b1 = s_b1 + fold(dp_rows)
            dp_b = dp_rows.astype(BF16)
            dp[rows, :] = dp_b
            dj = mm_nt(dp_b, w1[l]).astype(BF16)
            back = (c_rows + dj[:, :H].astype(F32)).astype(BF16)
            if l == 0:
                e_grad[0, rows, :] = back
            else:
                de[rows, :] = back
            dsq[rows, :] = dj[:, H:]
            return s_g, s_b2, s_b1

        zero = jnp.zeros((8, H), F32)
        dge, dbe2, dbe1 = lax.fori_loop(0, E // C, edge_back, (zero, zero, zero))
        def halo_cots():
            bsrc[l] = mm(ot_s[N:, :], dsq[:, :H]).astype(BF16)
            send_ret(l)

        if l > 0:
            halo_cots()
        if l + 1 < L:
            start_b(1, l + 1)
        dp_t = dp[...].T
        e_rows = edges[0] if l == 0 else e_in[l - 1]
        start_a(
            1,
            l,
            [mm(dp_t, e_rows).T, mm(dp_t, sq[l]).T, mm(dm[...].T, hid[l]).T]
            + [row_sum(v) for v in (dbe1, dbe2, dge)],
        )
        if l == 0:
            start_b(0, 0)
            halo_cots()
        if l + 1 < L:
            start_c(0, l + 1)
            start_c(1, l + 1)
        total = dx[...] + mm(ot_s[:N, :], dsq[:, :H]) + mm(ot_r[...], dsq[:, H:])
        wait_ret(l)
        x_cot = (total + mm(ot_x[...], ret[l])).astype(BF16)
    x_grad[0] = x_cot

    start_c(0, 0)
    start_b(1, 0)
    start_c(1, 0)
    for l in reversed(range(L)):
        for t in range(2):
            end_c(t, l)

    for l in range(L):
        for k in range(4):
            @pl.when(out_ok[k])
            def _(k=k, l=l):
                fcopy(l, k).wait_send()

            @pl.when(in_ok[k])
            def _(k=k, l=l):
                bcopy(l, k).wait_send()
        for t in range(2):
            for off in range(1, D):
                a_copy(t, l, off).wait_send()
                c_copy(t, l, off).wait_send()
            for off in range(1, G):
                b_copy(t, l, off).wait_send()


def finish(scale, H, x0, xg0, eg0, sum_n, sum_e, x1, xg1, eg1, g_w1, g_w2, g_n1, g_n2, g_b, g_g):
    x1[...] = x0[...]
    xg1[...] = xg0[...]
    eg1[...] = eg0[...]
    L, D, share_n, _ = sum_n.shape
    share_e = sum_e.shape[2]
    for l in range(L):
        node = (sum_n[l].astype(F32) * scale).reshape(D * share_n, H)
        edge = (sum_e[l].astype(F32) * scale).reshape(D * share_e, H)
        g_n1[l] = node[: 2 * H]
        g_n2[l] = node[2 * H : 3 * H]
        g_w1[l] = edge[: 3 * H]
        g_w2[l] = edge[3 * H : 4 * H]
        node = node[3 * H : 3 * H + 8]
        edge = edge[4 * H : 4 * H + 8]
        g_b[l, 0:2, :] = edge[0:2]
        g_b[l, 2:4, :] = node[0:2]
        g_g[l, 0:1, :] = edge[2:3]
        g_g[l, 1:2, :] = node[2:3]


def shards(D, G, nodes, edges, node_cot, send_index, halo_count, senders, receivers, *weights):
    edge_in_w, edge_out_w, node_in_w, node_out_w, biases, gains = weights
    _, N, H = nodes.shape
    E = edges.shape[1]
    L = edge_in_w.shape[0]
    HALO = send_index.shape[2]
    C = E // 2
    share_n = -(-(3 * H + 3) // (8 * D)) * 8
    share_e = -(-(4 * H + 3) // (8 * D)) * 8
    dims = (D, G, L, N, E, H, HALO, C, share_n, share_e)
    T = N + 4 * HALO
    own_shape = (
        pltpu.VMEM(nodes.shape, BF16),
        pltpu.VMEM(nodes.shape, BF16),
        pltpu.VMEM(edges.shape, BF16),
        pltpu.VMEM((L, D, share_n, H), BF16),
        pltpu.VMEM((L, D, share_e, H), BF16),
    )
    out_shape = (
        jax.ShapeDtypeStruct(nodes.shape, BF16),
        jax.ShapeDtypeStruct(nodes.shape, BF16),
        jax.ShapeDtypeStruct(edges.shape, BF16),
        jax.ShapeDtypeStruct(edge_in_w.shape, F32),
        jax.ShapeDtypeStruct(edge_out_w.shape, F32),
        jax.ShapeDtypeStruct(node_in_w.shape, F32),
        jax.ShapeDtypeStruct(node_out_w.shape, F32),
        jax.ShapeDtypeStruct(biases.shape, F32),
        jax.ShapeDtypeStruct(gains.shape, F32),
    )
    V = pltpu.VMEM
    dma = pltpu.SemaphoreType.DMA
    scratch = [
        V((E, T), BF16),
        V((T, E), BF16),
        V((E, N), BF16),
        V((N, E), BF16),
        V((4 * HALO, N), BF16),
        V((N, 4 * HALO), BF16),
        V((L, T, H), BF16),
        V((max(L - 1, 1), E, H), BF16),
        V((E, H), BF16),
        V((L, E, 2 * H), BF16),
        V((L, E, H), BF16),
        V((L, E, H), F32),
        V((L, E, H), F32),
        V((L, E, H), F32),
        V((L, N, 2 * H), BF16),
        V((L, N, H), BF16),
        V((L, N, H), F32),
        V((L, N, H), F32),
        V((L, N, H), F32),
        V((E, H), BF16),
        V((E, H), BF16),
        V((E, H), BF16),
        V((E, 2 * H), BF16),
        V((N, H), F32),
        V((N, H), BF16),
        V((L, 4 * HALO, H), BF16),
        V((L, 4 * HALO, H), BF16),
        V((L, 4 * HALO, H), BF16),
        V((L, D, share_n, H), BF16),
        V((L, max(D - 1, 1), share_n, H), BF16),
        V((L, G, share_n, H), BF16),
        V((L, D, share_e, H), BF16),
        V((L, max(D - 1, 1), share_e, H), BF16),
        V((L, G, share_e, H), BF16),
        dma((L, 4)),
        dma((L, 4)),
        dma((L, 4)),
        dma((L, 4)),
        dma((2, L, D)),
        dma((2, L, D)),
        dma((2, L, G)),
        dma((2, L, G)),
        dma((2, L, D)),
        dma((2, L, D)),
        pltpu.SMEM(halo_count.shape, jnp.int32),
    ]
    operands = (nodes, edges, node_cot, send_index, senders, receivers) + weights
    scratch += [V(x.shape, x.dtype) for x in operands] + [dma((13,))]
    vm = pl.BlockSpec(memory_space=pltpu.VMEM)
    hbm = pl.BlockSpec(memory_space=pltpu.HBM)
    own = pl.pallas_call(
        functools.partial(kernel, dims),
        out_shape=own_shape,
        in_specs=[hbm] * 13,
        out_specs=tuple([vm] * 5),
        scratch_shapes=scratch,
        compiler_params=pltpu.CompilerParams(
            collective_id=0, has_side_effects=True, vmem_limit_bytes=VMEM_MAIN
        ),
    )(
        halo_count,
        *operands,
    )
    scale = (D * G * N) ** (-0.5)
    return pl.pallas_call(
        functools.partial(finish, scale, H),
        out_shape=out_shape,
        in_specs=[vm] * 5,
        out_specs=tuple([vm] * 9),
        compiler_params=pltpu.CompilerParams(vmem_limit_bytes=8 * 1024 * 1024),
    )(*own)


def solution(mesh):
    part3 = P(("dom", "group"), None, None)
    part2 = P(("dom", "group"), None)
    in_specs = (part3, part3, part3, part3, part2, part2, part2) + (P(),) * 6
    out_specs = (part3, part3, part3) + (P(),) * 6
    body = functools.partial(shards, mesh.shape["dom"], mesh.shape["group"])
    return jax.shard_map(
        body, mesh=mesh, in_specs=in_specs, out_specs=out_specs, check_vma=False
    )
```
